512 devices in a mesh: replica: 64 (over z, y_hi, core), shard: 8 (over x, y_lo).
Axes of the slice: x: 4, y: 4 (y_hi: 2, y_lo: 2; y = y_hi * 2 + y_lo), z: 16, core: 2. Of those that a mesh axis runs over, the one named last changes fastest.
Arguments:
- frames_in: bfloat16 [512, 512, 768], P(('replica', 'shard')), may hold values from -6 to 6
- lengths: int32 [512], P(('replica', 'shard')), may hold values from 128 to 512, as said below
- up_weight: bfloat16 [768, 1536], P('shard'), may hold values from -0.21875 to 0.21875
- norm_gain: bfloat16 [768], P('shard'), may hold values from 0.25 to 1.75
- conv_kernel: bfloat16 [32, 768], P(None, 'shard'), may hold values from -1 to 1
- down_weight: bfloat16 [768, 768], P(None, 'shard'), may hold values from -0.21875 to 0.21875
- cotangent: bfloat16 [512, 512, 768], P(('replica', 'shard')), may hold values from -24 to 24
Outputs:
- result: bfloat16 [512, 512, 768], P(('replica', 'shard'))
- grad_in: bfloat16 [512, 512, 768], P(('replica', 'shard'))
- up_grad: float32 [768, 1536], P('shard')
- gain_grad: float32 [768], P('shard')
- kernel_grad: float32 [32, 768], P(None, 'shard')
- down_grad: float32 [768, 768], P(None, 'shard')
The draws below stay inside these ranges and needn't reach their ends.
Inputs may be any that keep to these rules, and one draw needn't show every extreme that they name: `lengths`: each length is a multiple of 128; utterance 0 has 512 frames.
All inputs are finite; a program needn't handle non-finite values.
Results may differ from the reference program's by a relative error of at most 0.017.
Values may be sent and summed in bfloat16 or wider, within the bound.
A program may use at most 64 MiB of HBM per device.

```python
import jax
import jax.numpy as jnp
from jax import lax

D = 768
C = 768
K = 32
L = 512
UTT = 512
N_REPLICA = 64
N_SHARD = 8


def draw_lengths(key, part):
    blocks = jax.random.randint(key, (UTT,), 1, L // 128 + 1)
    values = (blocks * 128).astype(jnp.int32)
    return values.at[0].set(L)


def spiked(values, key, source, target, shards_of, factor):
    owner, partner = [(jnp.arange(values.shape[axis_at]) // (values.shape[axis_at] // shards_of)).reshape([-1 if axis == axis_at else 1 for axis in range(values.ndim)]) for axis_at in (source, target)]
    chosen = jax.random.permutation(key, shards_of)[partner]
    strong = (owner == chosen) | (owner == (partner + shards_of // 2) % shards_of)
    return jnp.where(strong, factor * values, values)


def shard_levels(own_key, extent, cuts, least, largest):
    def one(axis_at, blocks):
        steps = jax.random.uniform(jax.random.fold_in(jax.random.fold_in(own_key, 6), axis_at), (blocks,), jnp.float32, least / len(cuts), largest / len(cuts))
        return jnp.repeat(jnp.exp(steps), extent[axis_at] // blocks).reshape((-1,) + (1,) * (len(extent) - axis_at - 1))

    level = one(*cuts[0])
    for cut in cuts[1:]:
        level = level * one(*cut)
    return level


def scatter_about(key, extent, scale, reach, shards=(), kind=jnp.bfloat16):
    array = scale * jax.random.normal(key, extent, jnp.float32)
    if shards:
        array = array * shard_levels(key, extent, shards, -0.22, 0.18)
    return jnp.clip(array, -reach, reach).astype(kind)


def gaussian_with(stream_key, extent, spread, bound, split, heavy, kind=jnp.bfloat16):
    values = spread * jax.random.normal(stream_key, extent, jnp.float32)
    if split:
        values = values * shard_levels(stream_key, extent, split, -0.22, 0.18)
    return jnp.clip(spiked(values, jax.random.fold_in(stream_key, 3), *heavy), -bound, bound).astype(kind)


def setup_inputs(seed: int = 0) -> dict:
    splits = jax.random.split(jax.random.key(seed), 8)
    frames_in = scatter_about(splits[0], (UTT, L, D), 1.0, 6.0, ((0, 512),))
    lengths = draw_lengths(jax.random.fold_in(splits[7], 71), 0)
    up_weight = scatter_about(splits[2], (D, 2 * C), D ** -0.5, 0.21875, ((0, 8),))
    norm_gain = jnp.clip(1.0 + 0.15 * jax.random.normal(splits[3], (D,), jnp.float32), 0.25, 1.75).astype(jnp.bfloat16)
    conv_kernel = scatter_about(splits[4], (K, C), K ** -0.5, 1.0, ((1, 8),))
    down_weight = scatter_about(splits[5], (C, D), C ** -0.5, 0.21875, ((1, 8),))
    cotangent = gaussian_with(splits[6], (UTT, L, D), 1.0, 24.0, ((0, 512),), (0, 2, 256, 6.0))
    return {"frames_in": frames_in, "lengths": lengths, "up_weight": up_weight, "norm_gain": norm_gain, "conv_kernel": conv_kernel, "down_weight": down_weight, "cotangent": cotangent}


EPS = 1e-05

def normalize(inputs):
    average = lax.optimization_barrier(jnp.mean(inputs, axis=1, keepdims=True))
    centred = inputs - average
    inv_std = lax.rsqrt(lax.optimization_barrier(jnp.mean(centred * centred, axis=1, keepdims=True)) + EPS)
    return (centred * inv_std, inv_std)

def depthwise(signal, taps_f, front, back):
    frames = signal.shape[1]
    padded = jnp.pad(signal, ((0, 0), (front, back), (0, 0)))
    total = jnp.zeros_like(signal)
    for offset in range(taps_f.shape[0]):
        total = total + taps_f[offset] * padded[:, offset:offset + frames]
    return total

def tap_grads(grad, signal, front, back):
    frames = signal.shape[1]
    padded = jnp.pad(signal, ((0, 0), (front, back), (0, 0)))
    return jnp.stack([lax.optimization_barrier(jnp.sum(grad * padded[:, offset:offset + frames], axis=(0, 1))) for offset in range(front + back + 1)])

def layer_pass(frames_in, lengths, up_weight, norm_gain, conv_kernel, down_weight, cotangent):
    utts, frames, width = frames_in.shape
    chans = conv_kernel.shape[1]
    count_taps = conv_kernel.shape[0]
    front = count_taps // 2
    back = count_taps - 1 - front
    row_count = utts * frames
    live = (jnp.arange(frames, dtype=jnp.int32)[None, :] < lengths[:, None]).astype(jnp.float32)
    live_col = live.reshape(row_count, 1)
    inputs = frames_in.reshape(row_count, width).astype(jnp.float32)
    normed, inv_std = normalize(inputs)
    gain_f = norm_gain.astype(jnp.float32)
    scaled = (normed * gain_f).astype(jnp.bfloat16)
    projected = jnp.dot(scaled, up_weight, preferred_element_type=jnp.float32)
    values_half = projected[:, :chans]
    gate_sig = jax.nn.sigmoid(projected[:, chans:])
    gated = (values_half * gate_sig * live_col).astype(jnp.bfloat16)
    taps_f = conv_kernel.astype(jnp.float32)
    gated_f = gated.astype(jnp.float32).reshape(utts, frames, chans)
    filtered = depthwise(gated_f, taps_f, front, back).reshape(row_count, chans)
    activated = (jax.nn.silu(filtered) * live_col).astype(jnp.bfloat16)
    mixed = jnp.dot(activated, down_weight, preferred_element_type=jnp.float32)
    result = (inputs + mixed).astype(jnp.bfloat16)
    upstream = cotangent.reshape(row_count, width)
    d_act = lax.dot_general(upstream, down_weight, (((1,), (1,)), ((), ())), preferred_element_type=jnp.float32)
    filt_sig = jax.nn.sigmoid(filtered)
    d_filt = d_act * live_col * filt_sig * (1.0 + filtered * (1.0 - filt_sig))
    d_filt3 = d_filt.reshape(utts, frames, chans)
    kernel_part = tap_grads(d_filt3, gated_f, front, back)
    d_gated = depthwise(d_filt3, taps_f[::-1], back, front).reshape(row_count, chans) * live_col
    d_proj = jnp.concatenate([d_gated * gate_sig, d_gated * values_half * gate_sig * (1.0 - gate_sig)], axis=1).astype(jnp.bfloat16)
    down_part = lax.dot_general(activated, upstream, (((0,), (0,)), ((), ())), preferred_element_type=jnp.float32)
    up_part = lax.dot_general(scaled, d_proj, (((0,), (0,)), ((), ())), preferred_element_type=jnp.float32)
    d_scaled = lax.dot_general(d_proj, up_weight, (((1,), (1,)), ((), ())), preferred_element_type=jnp.float32)
    gain_part = lax.optimization_barrier(jnp.sum(d_scaled * normed, axis=0))
    d_normed = d_scaled * gain_f
    d_inputs = inv_std * (d_normed - lax.optimization_barrier(jnp.mean(d_normed, axis=1, keepdims=True)) - normed * lax.optimization_barrier(jnp.mean(d_normed * normed, axis=1, keepdims=True)))
    grad_in = (upstream.astype(jnp.float32) + d_inputs).astype(jnp.bfloat16)
    return (result.reshape(utts, frames, width), grad_in.reshape(utts, frames, width), (up_part, gain_part, kernel_part, down_part))

def reference(frames_in, lengths, up_weight, norm_gain, conv_kernel, down_weight, cotangent):
    groups = N_REPLICA * N_SHARD
    per_dev = frames_in.shape[0] // groups
    frames = frames_in.shape[1]
    width = frames_in.shape[2]
    chans = conv_kernel.shape[1]
    blocks_in = frames_in.reshape(groups, per_dev, frames, width)
    blocks_len = lengths.reshape(groups, per_dev)
    blocks_cot = cotangent.reshape(groups, per_dev, frames, width)

    def step(carry, item):
        block_in, block_len, block_cot = item
        result, grad_in, parts = layer_pass(block_in, block_len, up_weight, norm_gain, conv_kernel, down_weight, block_cot)
        rounded = tuple((lax.optimization_barrier(part.astype(jnp.bfloat16)).astype(jnp.float32) for part in parts))
        return (tuple((total + piece for total, piece in zip(carry, rounded))), (result, grad_in))
    init = (jnp.zeros((width, 2 * chans), jnp.float32), jnp.zeros((width,), jnp.float32), jnp.zeros(conv_kernel.shape, jnp.float32), jnp.zeros((chans, width), jnp.float32))
    totals, (results, grads_in) = lax.scan(step, init, (blocks_in, blocks_len, blocks_cot))
    factor = 1.0 / jnp.sqrt(jnp.float32(frames_in.shape[0] * frames))
    up_grad, gain_grad, kernel_grad, down_grad = (total * factor for total in totals)
    return (results.reshape(frames_in.shape), grads_in.reshape(frames_in.shape), up_grad, gain_grad, kernel_grad, down_grad)
```

```python
import jax
import jax.numpy as jnp
from jax import lax
from jax.experimental import pallas as pl
from jax.experimental.pallas import tpu as pltpu
from jax.sharding import PartitionSpec as P

EPS = 1e-05
WIDE = 2432
CUT = 1280
MESH = pl.DeviceIdType.MESH


def place():
    rep, sh = lax.axis_index("replica"), lax.axis_index("shard")
    z, y_hi, core = rep // 4, (rep // 2) % 2, rep % 2
    x, y_lo = sh // 2, sh % 2
    return x, y_hi * 2 + y_lo, z, core


def device(x, y, z, core):
    return ((z * 2 + y // 2) * 2 + core, x * 2 + y % 2)


def greet(partners):
    barrier = pltpu.get_barrier_semaphore()
    for partner in partners:
        pl.semaphore_signal(barrier, inc=1, device_id=partner, device_id_type=MESH)
    pl.semaphore_wait(barrier, len(partners))


def gather_kernel(w_ref, out_ref, local_sem, send_sem, recv_sem):
    x, y, z, core = place()
    y_lo = y % 2
    xp, xm, x2 = (x + 1) % 4, (x + 3) % 4, (x + 2) % 4
    yp, ym = (y + 1) % 4, (y + 3) % 4
    to_xp, to_xm = device(xp, y, z, core), device(xm, y, z, core)
    to_yp, to_ym = device(x, yp, z, core), device(x, ym, z, core)
    to_sib = device(x, y, z, 1 - core)
    greet([to_xp, to_xm, to_yp, to_ym, to_sib])

    def rows(bx, byl):
        return pl.ds(pl.multiple_of((bx * 2 + byl) * 96 + core * 48, 16), 48)

    LO, HI, ALL = pl.ds(0, CUT), pl.ds(CUT, WIDE - CUT), pl.ds(0, WIDE)
    own = pl.multiple_of((x * 2 + y_lo) * 96, 16)
    local = pltpu.make_async_copy(w_ref, out_ref.at[pl.ds(own, 96)], local_sem)
    local.start()
    mine = pl.ds(pl.multiple_of(core * 48, 16), 48)
    sent = []

    def send(index, bx, byl, cols, target, own_block=False):
        dst = out_ref.at[rows(bx, byl), cols]
        src = w_ref.at[mine, cols] if own_block else dst
        copy = pltpu.make_async_remote_copy(
            src_ref=src, dst_ref=dst, send_sem=send_sem.at[index], recv_sem=recv_sem.at[index],
            device_id=target, device_id_type=MESH)
        copy.start()
        sent.append(copy)

    def arrive(index, bx, byl, cols):
        dst = out_ref.at[rows(bx, byl), cols]
        pltpu.make_async_remote_copy(
            src_ref=dst, dst_ref=dst, send_sem=send_sem.at[index], recv_sem=recv_sem.at[index],
            device_id=to_sib, device_id_type=MESH).wait_recv()

    oth = 1 - y_lo
    send(0, x, y_lo, ALL, to_xp, True)
    send(1, x, y_lo, ALL, to_xm, True)
    send(4, x, y_lo, LO, to_yp, True)
    send(8, x, y_lo, HI, to_ym, True)
    arrive(0, xm, y_lo, ALL)
    send(2, xm, y_lo, LO, to_xp)
    send(5, xm, y_lo, LO, to_yp)
    send(9, xm, y_lo, HI, to_ym)
    arrive(1, xp, y_lo, ALL)
    send(3, xp, y_lo, HI, to_xm)
    send(6, xp, y_lo, LO, to_yp)
    send(10, xp, y_lo, HI, to_ym)
    send(12, xm, y_lo, ALL, to_sib)
    send(13, xp, y_lo, ALL, to_sib)
    arrive(4, x, oth, LO)
    send(16, x, oth, LO, to_sib)
    arrive(8, x, oth, HI)
    send(20, x, oth, HI, to_sib)
    arrive(2, x2, y_lo, LO)
    send(7, x2, y_lo, LO, to_yp)
    send(14, x2, y_lo, LO, to_sib)
    arrive(3, x2, y_lo, HI)
    send(11, x2, y_lo, HI, to_ym)
    send(15, x2, y_lo, HI, to_sib)
    for k, bx in ((1, xm), (2, xp), (3, x2)):
        arrive(4 + k, bx, oth, LO)
        send(16 + k, bx, oth, LO, to_sib)
        arrive(8 + k, bx, oth, HI)
        send(20 + k, bx, oth, HI, to_sib)

    def sib_rows(bx, byl):
        return pl.ds(pl.multiple_of((bx * 2 + byl) * 96 + (1 - core) * 48, 16), 48)

    def arrive_sib(index, bx, byl, cols):
        dst = out_ref.at[sib_rows(bx, byl), cols]
        pltpu.make_async_remote_copy(
            src_ref=dst, dst_ref=dst, send_sem=send_sem.at[index], recv_sem=recv_sem.at[index],
            device_id=to_sib, device_id_type=MESH).wait_recv()

    arrive_sib(12, xm, y_lo, ALL)
    arrive_sib(13, xp, y_lo, ALL)
    arrive_sib(14, x2, y_lo, LO)
    arrive_sib(15, x2, y_lo, HI)
    for k, bx in ((0, x), (1, xm), (2, xp), (3, x2)):
        arrive_sib(16 + k, bx, oth, LO)
        arrive_sib(20 + k, bx, oth, HI)
    for copy in sent:
        copy.wait_send()
    local.wait()


def gather_weights(packed):
    return pl.pallas_call(
        gather_kernel,
        out_shape=jax.ShapeDtypeStruct((768, WIDE), jnp.bfloat16),
        in_specs=[pl.BlockSpec(memory_space=pltpu.VMEM)],
        out_specs=pl.BlockSpec(memory_space=pltpu.VMEM),
        scratch_shapes=[
            pltpu.SemaphoreType.DMA,
            pltpu.SemaphoreType.DMA((24,)),
            pltpu.SemaphoreType.DMA((24,)),
        ],
        compiler_params=pltpu.CompilerParams(collective_id=0, has_side_effects=True),
        name="gather_weights",
    )(packed)


def add_rows(rows, step, dst, terms):
    def one(i, carry):
        at = pl.ds(pl.multiple_of(i * step, 16), step)
        total = terms[0](at).astype(jnp.float32)
        for term in terms[1:]:
            total = total + term(at).astype(jnp.float32)
        dst(at, total)
        return carry

    lax.fori_loop(0, rows // step, one, 0)


def reduce_kernel(factor, g_ref, out_ref, cr, cs, xr, xq, xs, yr, yq, zs, zr, fin,
                  send_sem, recv_sem, zsend, zrecv, asend, arecv):
    x, y, z, core = place()
    y_lo, y_hi = y % 2, y // 2
    xp, xm, x2 = (x + 1) % 4, (x + 3) % 4, (x + 2) % 4
    yp, ym, y2 = (y + 1) % 4, (y + 3) % 4, (y + 2) % 4
    to_xp, to_xm = device(xp, y, z, core), device(xm, y, z, core)
    to_yp, to_ym = device(x, yp, z, core), device(x, ym, z, core)
    to_y2 = device(x, y2, z, core)
    to_sib = device(x, y, z, 1 - core)

    barrier = pltpu.get_barrier_semaphore()
    for partner in (to_xp, to_xm, to_yp, to_ym, to_y2, to_sib):
        pl.semaphore_signal(barrier, inc=1, device_id=partner, device_id_type=MESH)

    def hello(d, carry):
        pl.semaphore_signal(barrier, inc=1, device_id=device(x, y, (z + d) % 16, core), device_id_type=MESH)
        return carry

    lax.fori_loop(1, 16, hello, 0)
    pl.semaphore_wait(barrier, 21)
    sent = []

    def copy(index, src, dst, target):
        return pltpu.make_async_remote_copy(
            src_ref=src, dst_ref=dst, send_sem=send_sem.at[index], recv_sem=recv_sem.at[index],
            device_id=target, device_id_type=MESH)

    def send(index, src, dst, target):
        c = copy(index, src, dst, target)
        c.start()
        sent.append(c)

    def arrive(index, dst):
        copy(index, dst, dst, to_sib).wait_recv()

    order = (x2, xp, xm, x)
    for k, bx in enumerate(order):
        send(k, g_ref.at[bx, :, 1 - core], cr.at[bx], to_sib)
    def core_sum(k):
        bx = order[k]
        arrive(k, cr.at[bx])
        for j in range(2):
            def put(at, v):
                cs[bx, j, at, :] = v.astype(jnp.bfloat16)
            add_rows(896, 128, put, [lambda at: g_ref[bx, j, core, at, :], lambda at: cr[bx, j, at, :]])

    core_sum(0)
    send(4, cs.at[x2, 0], xq.at[0], to_xp)
    send(5, cs.at[x2, 1], xq.at[1], to_xm)
    core_sum(1)
    send(6, cs.at[xp, 1], xr.at[0, 1], to_xp)
    core_sum(2)
    send(7, cs.at[xm, 0], xr.at[1, 0], to_xm)
    arrive(4, xq.at[0])

    def put_p(at, v):
        cs[xp, 0, at, :] = v.astype(jnp.bfloat16)

    add_rows(896, 128, put_p, [lambda at: cs[xp, 0, at, :], lambda at: xq[0, at, :]])
    send(8, cs.at[xp, 0], xr.at[0, 0], to_xp)
    arrive(5, xq.at[1])

    def put_m(at, v):
        cs[xm, 1, at, :] = v.astype(jnp.bfloat16)

    add_rows(896, 128, put_m, [lambda at: cs[xm, 1, at, :], lambda at: xq[1, at, :]])
    send(9, cs.at[xm, 1], xr.at[1, 1], to_xm)
    core_sum(3)
    arrive(6, xr.at[0, 1])
    arrive(7, xr.at[1, 0])
    arrive(8, xr.at[0, 0])
    arrive(9, xr.at[1, 1])
    for j in range(2):
        def put(at, v):
            xs[j, at, :] = v.astype(jnp.bfloat16)
        add_rows(896, 128, put, [lambda at: cs[x, j, at, :], lambda at: xr[0, j, at, :], lambda at: xr[1, j, at, :]])

    def part(yy, half, rows=224):
        return xs.at[yy % 2, pl.ds(pl.multiple_of((yy // 2) * 448 + half * 224, 16), rows)]

    send(10, part(y2, 0), yq.at[0], to_yp)
    send(11, part(y2, 1), yq.at[1], to_ym)
    send(12, part(yp, 1), yr.at[0, 1], to_yp)
    send(13, part(ym, 0), yr.at[1, 0], to_ym)
    arrive(10, yq.at[0])
    dst_p = part(yp, 0)

    def put_yp(at, v):
        dst_p[at, :] = v.astype(jnp.bfloat16)

    add_rows(224, 32, put_yp, [lambda at: dst_p[at, :], lambda at: yq[0, at, :]])
    send(14, part(yp, 0), yr.at[0, 0], to_yp)
    arrive(11, yq.at[1])
    dst_m = part(ym, 1)

    def put_ym(at, v):
        dst_m[at, :] = v.astype(jnp.bfloat16)

    add_rows(224, 32, put_ym, [lambda at: dst_m[at, :], lambda at: yq[1, at, :]])
    send(15, part(ym, 1), yr.at[1, 1], to_ym)
    arrive(12, yr.at[0, 1])
    arrive(13, yr.at[1, 0])
    arrive(14, yr.at[0, 0])
    arrive(15, yr.at[1, 1])
    zs[pl.ds(448, 64), :] = jnp.zeros((64, 128), jnp.bfloat16)
    for half in range(2):
        mine = part(y, half)

        def put(at, v):
            zs[pl.ds(pl.multiple_of(half * 224 + at.start, 16), 32), :] = v.astype(jnp.bfloat16)

        add_rows(224, 32, put, [lambda at: mine[at, :], lambda at: yr[0, half, at, :], lambda at: yr[1, half, at, :]])

    def piece(p):
        return pl.ds(pl.multiple_of(p * 32, 32), 32)

    def z_copy(d):
        to = (z + d) % 16
        return pltpu.make_async_remote_copy(
            src_ref=zs.at[piece(to)], dst_ref=zr.at[d], send_sem=zsend.at[d], recv_sem=zrecv.at[d],
            device_id=device(x, y, to, core), device_id_type=MESH)

    def z_start(d, carry):
        z_copy(d).start()
        return carry

    lax.fori_loop(1, 16, z_start, 0)

    def z_add(d, total):
        z_copy(d).wait_recv()
        return total + zr[d].astype(jnp.float32)

    total = lax.fori_loop(1, 16, z_add, zs[piece(z), :].astype(jnp.float32))
    mine_at = fin.at[core, y_hi]
    mine_at[piece(z), :] = total.astype(jnp.bfloat16)

    def a_copy(d, p):
        at = fin.at[core, y_hi, piece(p)]
        return pltpu.make_async_remote_copy(
            src_ref=at, dst_ref=at, send_sem=asend.at[d], recv_sem=arecv.at[d],
            device_id=device(x, y, (z + d) % 16, core), device_id_type=MESH)

    def a_start(d, carry):
        a_copy(d, z).start()
        return carry

    lax.fori_loop(1, 16, a_start, 0)

    def a_wait(d, carry):
        a_copy(d, (z + 16 - d) % 16).wait_recv()
        return carry

    lax.fori_loop(1, 16, a_wait, 0)
    both = fin.at[core, y_hi, pl.ds(0, 448)]
    send(16, both, both, to_y2)
    send(17, both, both, to_sib)
    far = fin.at[core, 1 - y_hi, pl.ds(0, 448)]
    arrive(16, far)
    send(18, far, far, to_sib)

    def z_done(d, carry):
        z_copy(d).wait_send()
        a_copy(d, z).wait_send()
        return carry

    lax.fori_loop(1, 16, z_done, 0)
    arrive(17, fin.at[1 - core, y_hi, pl.ds(0, 448)])
    arrive(18, fin.at[1 - core, 1 - y_hi, pl.ds(0, 448)])
    for c in range(2):
        for h in range(2):
            def put(at, v):
                out_ref[c, h, at, :] = v * factor
            add_rows(448, 64, put, [lambda at: fin[c, h, at, :]])
    for c in sent:
        c.wait_send()


def reduce_parts(packed, factor):
    bf = jnp.bfloat16
    return pl.pallas_call(
        lambda *refs: reduce_kernel(factor, *refs),
        out_shape=jax.ShapeDtypeStruct((2, 2, 448, 128), jnp.float32),
        in_specs=[pl.BlockSpec(memory_space=pltpu.VMEM)],
        out_specs=pl.BlockSpec(memory_space=pltpu.VMEM),
        scratch_shapes=[
            pltpu.VMEM((4, 2, 896, 128), bf),
            pltpu.VMEM((4, 2, 896, 128), bf),
            pltpu.VMEM((2, 2, 896, 128), bf),
            pltpu.VMEM((2, 896, 128), bf),
            pltpu.VMEM((2, 896, 128), bf),
            pltpu.VMEM((2, 2, 224, 128), bf),
            pltpu.VMEM((2, 224, 128), bf),
            pltpu.VMEM((512, 128), bf),
            pltpu.VMEM((16, 32, 128), bf),
            pltpu.VMEM((2, 2, 512, 128), bf),
            pltpu.SemaphoreType.DMA((19,)),
            pltpu.SemaphoreType.DMA((19,)),
            pltpu.SemaphoreType.DMA((16,)),
            pltpu.SemaphoreType.DMA((16,)),
            pltpu.SemaphoreType.DMA((16,)),
            pltpu.SemaphoreType.DMA((16,)),
        ],
        compiler_params=pltpu.CompilerParams(collective_id=1, has_side_effects=True),
        name="reduce_parts",
    )(packed)


def tiles(array, columns):
    return array.reshape(8, 12, 8, columns, 128).transpose(0, 1, 3, 2, 4).reshape(8, 12 * columns, 8, 128)


def untiles(array, columns):
    return array.reshape(12, columns, 8, 128).transpose(0, 2, 1, 3).reshape(96, columns * 128)


def normalize(inputs):
    average = jnp.mean(inputs, axis=1, keepdims=True)
    centred = inputs - average
    inv_std = lax.rsqrt(jnp.mean(centred * centred, axis=1, keepdims=True) + EPS)
    return (centred * inv_std, inv_std)


def depthwise(signal, taps_f, front, back):
    frames = signal.shape[1]
    padded = jnp.pad(signal, ((0, 0), (front, back), (0, 0)))
    total = jnp.zeros_like(signal)
    for offset in range(taps_f.shape[0]):
        total = total + taps_f[offset] * padded[:, offset : offset + frames]
    return total


def tap_grads(grad, signal, front, back):
    frames = signal.shape[1]
    padded = jnp.pad(signal, ((0, 0), (front, back), (0, 0)))
    return jnp.stack(
        [
            jnp.sum(grad * padded[:, offset : offset + frames], axis=(0, 1))
            for offset in range(front + back + 1)
        ]
    )


def body(frames_in, lengths, up_weight, norm_gain, conv_kernel, down_weight, cotangent):
    utts, frames, width = frames_in.shape
    chans = up_weight.shape[1] // 2
    count_taps = conv_kernel.shape[0]
    front = count_taps // 2
    back = count_taps - 1 - front
    row_count = utts * frames
    bf = jnp.bfloat16
    packed = jnp.concatenate(
        [up_weight, down_weight.T, conv_kernel.T, norm_gain[:, None], jnp.zeros((96, 95), bf)], axis=1
    )
    full = gather_weights(packed)
    up_full = full[:, :1536]
    down_t = full[:, 1536:2304]
    small = full[:, 2304:].T
    taps_bf, gain_bf = small[:32], small[32]

    live = (jnp.arange(frames, dtype=jnp.int32)[None, :] < lengths[:, None]).astype(jnp.float32)
    live_col = live.reshape(row_count, 1)
    inputs = frames_in.reshape(row_count, width).astype(jnp.float32)
    normed, inv_std = normalize(inputs)
    gain_f = gain_bf.astype(jnp.float32)
    scaled = (normed * gain_f).astype(bf)
    projected = jnp.dot(scaled, up_full, preferred_element_type=jnp.float32)
    values_half = projected[:, :chans]
    gate_sig = jax.nn.sigmoid(projected[:, chans:])
    gated = (values_half * gate_sig * live_col).astype(bf)
    taps_f = taps_bf.astype(jnp.float32)
    gated_f = gated.astype(jnp.float32).reshape(utts, frames, chans)
    filtered = depthwise(gated_f, taps_f, front, back).reshape(row_count, chans)
    activated = (jax.nn.silu(filtered) * live_col).astype(bf)
    upstream = cotangent.reshape(row_count, width)
    mixed = lax.dot_general(
        activated, down_t, (((1,), (1,)), ((), ())), preferred_element_type=jnp.float32
    )
    d_act = jnp.dot(upstream, down_t, preferred_element_type=jnp.float32)
    result = (inputs + mixed).astype(bf)
    down_part = lax.dot_general(
        upstream, activated, (((0,), (0,)), ((), ())), preferred_element_type=jnp.float32
    )
    factor = 1.0 / float(utts * 512 * frames) ** 0.5
    filt_sig = jax.nn.sigmoid(filtered)
    d_filt = d_act * live_col * filt_sig * (1.0 + filtered * (1.0 - filt_sig))
    d_filt3 = d_filt.reshape(utts, frames, chans)
    kernel_part = tap_grads(d_filt3, gated_f, front, back)
    d_gated = depthwise(d_filt3, taps_f[::-1], back, front).reshape(row_count, chans) * live_col
    d_proj = jnp.concatenate(
        [d_gated * gate_sig, d_gated * values_half * gate_sig * (1.0 - gate_sig)], axis=1
    ).astype(bf)
    up_part = lax.dot_general(
        scaled, d_proj, (((0,), (0,)), ((), ())), preferred_element_type=jnp.float32
    )
    d_scaled = lax.dot_general(
        d_proj, up_full, (((1,), (1,)), ((), ())), preferred_element_type=jnp.float32
    )
    gain_part = jnp.sum(d_scaled * normed, axis=0)
    d_normed = d_scaled * gain_f
    d_inputs = inv_std * (
        d_normed
        - jnp.mean(d_normed, axis=1, keepdims=True)
        - normed * jnp.mean(d_normed * normed, axis=1, keepdims=True)
    )
    grad_in = (upstream.astype(jnp.float32) + d_inputs).astype(bf)

    taps_tiles = jnp.pad(
        kernel_part.astype(bf).reshape(32, 8, 96).transpose(1, 0, 2), ((0, 0), (0, 0), (0, 32))
    ).reshape(8, 4, 8, 128)
    gain_tiles = jnp.pad(
        gain_part.astype(bf).reshape(8, 1, 1, 96), ((0, 0), (0, 3), (0, 7), (0, 32))
    )
    parts = jnp.concatenate(
        [tiles(up_part.astype(bf), 12), tiles(down_part.astype(bf), 6), taps_tiles, gain_tiles], axis=1
    ).reshape(4, 2, 2, 896, 128)
    total = reduce_parts(parts, factor).reshape(224, 8, 128)
    up_total = untiles(total[:144], 12)
    down_total = untiles(total[144:216], 6).T
    kernel_total = total[216:220].reshape(32, 128)[:, :96]
    gain_total = total[220, 0, :96]
    return (
        result.reshape(utts, frames, width),
        grad_in.reshape(utts, frames, width),
        up_total,
        gain_total,
        kernel_total,
        down_total,
    )


def solution(mesh):
    return jax.shard_map(
        body,
        mesh=mesh,
        in_specs=(
            P(("replica", "shard"), None, None),
            P(("replica", "shard")),
            P("shard", None),
            P("shard"),
            P(None, "shard"),
            P(None, "shard"),
            P(("replica", "shard"), None, None),
        ),
        out_specs=(
            P(("replica", "shard"), None, None),
            P(("replica", "shard"), None, None),
            P("shard", None),
            P("shard"),
            P(None, "shard"),
            P(None, "shard"),
        ),
        check_vma=False,
    )
```

```python
import functools

import jax
import jax.numpy as jnp
from jax import lax
from jax.experimental import pallas as pl
from jax.experimental.pallas import tpu as pltpu
from jax.sharding import PartitionSpec as P

EPS = 1e-05
WIDE = 2432
CUT = 1280
MESH = pl.DeviceIdType.MESH


def place():
    rep, sh = lax.axis_index("replica"), lax.axis_index("shard")
    z, y_hi, core = rep // 4, (rep // 2) % 2, rep % 2
    x, y_lo = sh // 2, sh % 2
    return x, y_hi * 2 + y_lo, z, core


def device(x, y, z, core):
    return ((z * 2 + y // 2) * 2 + core, x * 2 + y % 2)


def greet(partners):
    barrier = pltpu.get_barrier_semaphore()
    for partner in partners:
        pl.semaphore_signal(barrier, inc=1, device_id=partner, device_id_type=MESH)
    pl.semaphore_wait(barrier, len(partners))


def gather_kernel(w_ref, out_ref, local_sem, send_sem, recv_sem):
    x, y, z, core = place()
    y_lo = y % 2
    xp, xm, x2 = (x + 1) % 4, (x + 3) % 4, (x + 2) % 4
    yp, ym = (y + 1) % 4, (y + 3) % 4
    to_xp, to_xm = device(xp, y, z, core), device(xm, y, z, core)
    to_yp, to_ym = device(x, yp, z, core), device(x, ym, z, core)
    to_sib = device(x, y, z, 1 - core)
    greet([to_xp, to_xm, to_yp, to_ym, to_sib])

    def rows(bx, byl):
        return pl.ds(pl.multiple_of((bx * 2 + byl) * 96 + core * 48, 16), 48)

    LO, HI, ALL = pl.ds(0, CUT), pl.ds(CUT, WIDE - CUT), pl.ds(0, WIDE)
    own = pl.multiple_of((x * 2 + y_lo) * 96, 16)
    local = pltpu.make_async_copy(w_ref, out_ref.at[pl.ds(own, 96)], local_sem)
    local.start()
    mine = pl.ds(pl.multiple_of(core * 48, 16), 48)
    sent = []

    def send(index, bx, byl, cols, target, own_block=False):
        dst = out_ref.at[rows(bx, byl), cols]
        src = w_ref.at[mine, cols] if own_block else dst
        copy = pltpu.make_async_remote_copy(
            src_ref=src, dst_ref=dst, send_sem=send_sem.at[index], recv_sem=recv_sem.at[index],
            device_id=target, device_id_type=MESH)
        copy.start()
        sent.append(copy)

    def arrive(index, bx, byl, cols):
        dst = out_ref.at[rows(bx, byl), cols]
        pltpu.make_async_remote_copy(
            src_ref=dst, dst_ref=dst, send_sem=send_sem.at[index], recv_sem=recv_sem.at[index],
            device_id=to_sib, device_id_type=MESH).wait_recv()

    oth = 1 - y_lo
    send(0, x, y_lo, ALL, to_xp, True)
    send(1, x, y_lo, ALL, to_xm, True)
    send(4, x, y_lo, LO, to_yp, True)
    send(8, x, y_lo, HI, to_ym, True)
    arrive(0, xm, y_lo, ALL)
    send(2, xm, y_lo, LO, to_xp)
    send(5, xm, y_lo, LO, to_yp)
    send(9, xm, y_lo, HI, to_ym)
    arrive(1, xp, y_lo, ALL)
    send(3, xp, y_lo, HI, to_xm)
    send(6, xp, y_lo, LO, to_yp)
    send(10, xp, y_lo, HI, to_ym)
    send(12, xm, y_lo, ALL, to_sib)
    send(13, xp, y_lo, ALL, to_sib)
    arrive(4, x, oth, LO)
    send(16, x, oth, LO, to_sib)
    arrive(8, x, oth, HI)
    send(20, x, oth, HI, to_sib)
    arrive(2, x2, y_lo, LO)
    send(7, x2, y_lo, LO, to_yp)
    send(14, x2, y_lo, LO, to_sib)
    arrive(3, x2, y_lo, HI)
    send(11, x2, y_lo, HI, to_ym)
    send(15, x2, y_lo, HI, to_sib)
    for k, bx in ((1, xm), (2, xp), (3, x2)):
        arrive(4 + k, bx, oth, LO)
        send(16 + k, bx, oth, LO, to_sib)
        arrive(8 + k, bx, oth, HI)
        send(20 + k, bx, oth, HI, to_sib)

    def sib_rows(bx, byl):
        return pl.ds(pl.multiple_of((bx * 2 + byl) * 96 + (1 - core) * 48, 16), 48)

    def arrive_sib(index, bx, byl, cols):
        dst = out_ref.at[sib_rows(bx, byl), cols]
        pltpu.make_async_remote_copy(
            src_ref=dst, dst_ref=dst, send_sem=send_sem.at[index], recv_sem=recv_sem.at[index],
            device_id=to_sib, device_id_type=MESH).wait_recv()

    arrive_sib(12, xm, y_lo, ALL)
    arrive_sib(13, xp, y_lo, ALL)
    arrive_sib(14, x2, y_lo, LO)
    arrive_sib(15, x2, y_lo, HI)
    for k, bx in ((0, x), (1, xm), (2, xp), (3, x2)):
        arrive_sib(16 + k, bx, oth, LO)
        arrive_sib(20 + k, bx, oth, HI)
    for copy in sent:
        copy.wait_send()
    local.wait()


def gather_weights(packed):
    return pl.pallas_call(
        gather_kernel,
        out_shape=jax.ShapeDtypeStruct((768, WIDE), jnp.bfloat16),
        in_specs=[pl.BlockSpec(memory_space=pltpu.VMEM)],
        out_specs=pl.BlockSpec(memory_space=pltpu.VMEM),
        scratch_shapes=[
            pltpu.SemaphoreType.DMA,
            pltpu.SemaphoreType.DMA((24,)),
            pltpu.SemaphoreType.DMA((24,)),
        ],
        compiler_params=pltpu.CompilerParams(collective_id=0, has_side_effects=True),
        name="gather_weights",
    )(packed)


def add_rows(rows, step, dst, terms):
    def one(i, carry):
        at = pl.ds(pl.multiple_of(i * step, 16), step)
        total = terms[0](at).astype(jnp.float32)
        for term in terms[1:]:
            total = total + term(at).astype(jnp.float32)
        dst(at, total)
        return carry

    lax.fori_loop(0, rows // step, one, 0)


def reduce_kernel(factor, g_ref, up_ref, down_ref, rest_ref, cr, cs, xr, xq, xs, yr, yq, zs, zr, fin,
                  send_sem, recv_sem, zsend, zrecv, asend, arecv):
    x, y, z, core = place()
    y_lo, y_hi = y % 2, y // 2
    xp, xm, x2 = (x + 1) % 4, (x + 3) % 4, (x + 2) % 4
    yp, ym, y2 = (y + 1) % 4, (y + 3) % 4, (y + 2) % 4
    to_xp, to_xm = device(xp, y, z, core), device(xm, y, z, core)
    to_yp, to_ym = device(x, yp, z, core), device(x, ym, z, core)
    to_y2 = device(x, y2, z, core)
    to_sib = device(x, y, z, 1 - core)

    barrier = pltpu.get_barrier_semaphore()
    for partner in (to_xp, to_xm, to_yp, to_ym, to_y2, to_sib):
        pl.semaphore_signal(barrier, inc=1, device_id=partner, device_id_type=MESH)

    def hello(d, carry):
        pl.semaphore_signal(barrier, inc=1, device_id=device(x, y, (z + d) % 16, core), device_id_type=MESH)
        return carry

    lax.fori_loop(1, 16, hello, 0)
    pl.semaphore_wait(barrier, 21)
    sent = []

    def copy(index, src, dst, target):
        return pltpu.make_async_remote_copy(
            src_ref=src, dst_ref=dst, send_sem=send_sem.at[index], recv_sem=recv_sem.at[index],
            device_id=target, device_id_type=MESH)

    def send(index, src, dst, target):
        c = copy(index, src, dst, target)
        c.start()
        sent.append(c)

    def arrive(index, dst):
        copy(index, dst, dst, to_sib).wait_recv()

    order = (x2, xp, xm, x)
    for k, bx in enumerate(order):
        send(k, g_ref.at[bx, :, 1 - core], cr.at[bx], to_sib)
    def core_sum(k):
        bx = order[k]
        arrive(k, cr.at[bx])
        for j in range(2):
            def put(at, v):
                cs[bx, j, at, :] = v.astype(jnp.bfloat16)
            add_rows(896, 128, put, [lambda at: g_ref[bx, j, core, at, :], lambda at: cr[bx, j, at, :]])

    core_sum(0)
    send(4, cs.at[x2, 0], xq.at[0], to_xp)
    send(5, cs.at[x2, 1], xq.at[1], to_xm)
    core_sum(1)
    send(6, cs.at[xp, 1], xr.at[0, 1], to_xp)
    core_sum(2)
    send(7, cs.at[xm, 0], xr.at[1, 0], to_xm)
    arrive(4, xq.at[0])

    def put_p(at, v):
        cs[xp, 0, at, :] = v.astype(jnp.bfloat16)

    add_rows(896, 128, put_p, [lambda at: cs[xp, 0, at, :], lambda at: xq[0, at, :]])
    send(8, cs.at[xp, 0], xr.at[0, 0], to_xp)
    arrive(5, xq.at[1])

    def put_m(at, v):
        cs[xm, 1, at, :] = v.astype(jnp.bfloat16)

    add_rows(896, 128, put_m, [lambda at: cs[xm, 1, at, :], lambda at: xq[1, at, :]])
    send(9, cs.at[xm, 1], xr.at[1, 1], to_xm)
    core_sum(3)
    arrive(6, xr.at[0, 1])
    arrive(7, xr.at[1, 0])
    arrive(8, xr.at[0, 0])
    arrive(9, xr.at[1, 1])
    for j in range(2):
        def put(at, v):
            xs[j, at, :] = v.astype(jnp.bfloat16)
        add_rows(896, 128, put, [lambda at: cs[x, j, at, :], lambda at: xr[0, j, at, :], lambda at: xr[1, j, at, :]])

    def part(yy, half, rows=224):
        return xs.at[yy % 2, pl.ds(pl.multiple_of((yy // 2) * 448 + half * 224, 16), rows)]

    send(10, part(y2, 0), yq.at[0], to_yp)
    send(11, part(y2, 1), yq.at[1], to_ym)
    send(12, part(yp, 1), yr.at[0, 1], to_yp)
    send(13, part(ym, 0), yr.at[1, 0], to_ym)
    arrive(10, yq.at[0])
    dst_p = part(yp, 0)

    def put_yp(at, v):
        dst_p[at, :] = v.astype(jnp.bfloat16)

    add_rows(224, 32, put_yp, [lambda at: dst_p[at, :], lambda at: yq[0, at, :]])
    send(14, part(yp, 0), yr.at[0, 0], to_yp)
    arrive(11, yq.at[1])
    dst_m = part(ym, 1)

    def put_ym(at, v):
        dst_m[at, :] = v.astype(jnp.bfloat16)

    add_rows(224, 32, put_ym, [lambda at: dst_m[at, :], lambda at: yq[1, at, :]])
    send(15, part(ym, 1), yr.at[1, 1], to_ym)
    arrive(12, yr.at[0, 1])
    arrive(13, yr.at[1, 0])
    arrive(14, yr.at[0, 0])
    arrive(15, yr.at[1, 1])
    zs[pl.ds(448, 64), :] = jnp.zeros((64, 128), jnp.bfloat16)
    for half in range(2):
        mine = part(y, half)

        def put(at, v):
            zs[pl.ds(pl.multiple_of(half * 224 + at.start, 16), 32), :] = v.astype(jnp.bfloat16)

        add_rows(224, 32, put, [lambda at: mine[at, :], lambda at: yr[0, half, at, :], lambda at: yr[1, half, at, :]])

    def piece(p):
        return pl.ds(pl.multiple_of(p * 32, 32), 32)

    def z_copy(d):
        to = (z + d) % 16
        return pltpu.make_async_remote_copy(
            src_ref=zs.at[piece(to)], dst_ref=zr.at[d], send_sem=zsend.at[d], recv_sem=zrecv.at[d],
            device_id=device(x, y, to, core), device_id_type=MESH)

    def z_start(d, carry):
        z_copy(d).start()
        return carry

    lax.fori_loop(1, 16, z_start, 0)

    def z_add(d, total):
        z_copy(d).wait_recv()
        return total + zr[d].astype(jnp.float32)

    total = lax.fori_loop(1, 16, z_add, zs[piece(z), :].astype(jnp.float32))
    mine_at = fin.at[core, y_hi]
    mine_at[piece(z), :] = total.astype(jnp.bfloat16)

    def a_copy(d, p):
        at = fin.at[core, y_hi, piece(p)]
        return pltpu.make_async_remote_copy(
            src_ref=at, dst_ref=at, send_sem=asend.at[d], recv_sem=arecv.at[d],
            device_id=device(x, y, (z + d) % 16, core), device_id_type=MESH)

    def a_start(d, carry):
        a_copy(d, z).start()
        return carry

    lax.fori_loop(1, 16, a_start, 0)

    def a_wait(d, carry):
        a_copy(d, (z + 16 - d) % 16).wait_recv()
        return carry

    lax.fori_loop(1, 16, a_wait, 0)
    both = fin.at[core, y_hi, pl.ds(0, 448)]
    send(16, both, both, to_y2)
    send(17, both, both, to_sib)
    far = fin.at[core, 1 - y_hi, pl.ds(0, 448)]
    arrive(16, far)
    send(18, far, far, to_sib)

    def z_done(d, carry):
        z_copy(d).wait_send()
        a_copy(d, z).wait_send()
        return carry

    lax.fori_loop(1, 16, z_done, 0)
    arrive(17, fin.at[1 - core, y_hi, pl.ds(0, 448)])
    arrive(18, fin.at[1 - core, 1 - y_hi, pl.ds(0, 448)])
    def tile(row):
        at = row % 448
        return fin[row // 896, (row % 896) // 448, pl.ds(at, 16), :].astype(jnp.float32) * factor

    for rt in range(6):
        for ct in range(12):
            up_ref[pl.ds(rt * 16, 16), pl.ds(ct * 128, 128)] = tile((rt * 12 + ct) * 16)
        for ct in range(6):
            down_ref[pl.ds(rt * 16, 16), pl.ds(ct * 128, 128)] = tile(1152 + (rt * 6 + ct) * 16)
    for k in range(3):
        rest_ref[pl.ds(k * 16, 16), :] = tile(1728 + k * 16)
    for c in sent:
        c.wait_send()


def reduce_parts(packed, factor):
    bf = jnp.bfloat16
    return pl.pallas_call(
        lambda *refs: reduce_kernel(factor, *refs),
        out_shape=(
            jax.ShapeDtypeStruct((96, 1536), jnp.float32),
            jax.ShapeDtypeStruct((96, 768), jnp.float32),
            jax.ShapeDtypeStruct((48, 128), jnp.float32),
        ),
        in_specs=[pl.BlockSpec(memory_space=pltpu.VMEM)],
        out_specs=(pl.BlockSpec(memory_space=pltpu.VMEM),) * 3,
        scratch_shapes=[
            pltpu.VMEM((4, 2, 896, 128), bf),
            pltpu.VMEM((4, 2, 896, 128), bf),
            pltpu.VMEM((2, 2, 896, 128), bf),
            pltpu.VMEM((2, 896, 128), bf),
            pltpu.VMEM((2, 896, 128), bf),
            pltpu.VMEM((2, 2, 224, 128), bf),
            pltpu.VMEM((2, 224, 128), bf),
            pltpu.VMEM((512, 128), bf),
            pltpu.VMEM((16, 32, 128), bf),
            pltpu.VMEM((2, 2, 512, 128), bf),
            pltpu.SemaphoreType.DMA((19,)),
            pltpu.SemaphoreType.DMA((19,)),
            pltpu.SemaphoreType.DMA((16,)),
            pltpu.SemaphoreType.DMA((16,)),
            pltpu.SemaphoreType.DMA((16,)),
            pltpu.SemaphoreType.DMA((16,)),
        ],
        compiler_params=pltpu.CompilerParams(collective_id=1, has_side_effects=True),
        name="reduce_parts",
    )(packed)


def layer_kernel(len_ref, x_ref, ct_ref, upv_ref, upg_ref, dt_ref, taps_ref, gain_ref,
                 res_ref, gin_ref, g_ref,
                 normed, invs, scaled, scaled_t, cot_t, vals, gsig, dact, gat, dfl, act, dpv, dpg,
                 mixed, dsc, kacc, kall):
    i = pl.program_id(0)
    f32, bf = jnp.float32, jnp.bfloat16
    length = len_ref[0]

    def live_of(base, rows):
        return ((lax.broadcasted_iota(jnp.int32, (rows, 128), 0) + base) < length).astype(f32)

    @pl.when(i == 0)
    def _():
        gain = gain_ref[...]

        def norm(c, carry):
            at = pl.ds(pl.multiple_of(c * 32, 32), 32)
            v = x_ref[at, :].astype(f32)
            centred = v - jnp.mean(v, axis=1, keepdims=True)
            inv = lax.rsqrt(jnp.mean(centred * centred, axis=1, keepdims=True) + EPS)
            n = centred * inv
            normed[at, :] = n
            invs[at, :] = jnp.broadcast_to(inv, (32, 128))
            scaled[at, :] = (n * gain).astype(bf)
            return carry

        lax.fori_loop(0, 16, norm, 0)
        scaled_t[...] = scaled[...].T
        cot_t[...] = ct_ref[...].T
        for buf in (gat, dfl):
            for h in range(2):
                buf[h, pl.ds(0, 16), :] = jnp.zeros((16, 128), f32)
                buf[h, pl.ds(528, 16), :] = jnp.zeros((16, 128), f32)
        for s in range(8):
            g_ref[s, pl.ds(1728, 64), :] = jnp.zeros((64, 128), bf)

    dot = functools.partial(lax.dot_general, preferred_element_type=f32)
    NN, NT = (((1,), (0,)), ((), ())), (((1,), (1,)), ((), ()))

    def gate(c, carry):
        base = pl.multiple_of(c * 128, 128)
        at = pl.ds(base, 128)
        live = live_of(base, 128)
        v = dot(scaled[at, :], upv_ref[...], NN)
        sg = jax.nn.sigmoid(dot(scaled[at, :], upg_ref[...], NN))
        vals[at, :] = v
        gsig[at, :] = sg
        dact[at, :] = dot(ct_ref[at, :], dt_ref[...], NN)
        for h in range(2):
            cols = slice(h * 128, h * 128 + 128)
            gat[h, pl.ds(base + 16, 128), :] = (v[:, cols] * sg[:, cols] * live).astype(bf).astype(f32)
        return carry

    lax.fori_loop(0, 4, gate, 0)
    R = 64
    for h in range(2):
        cols = pl.ds(h * 128, 128)
        kacc[...] = jnp.zeros_like(kacc)

        def forward(c, carry):
            base = pl.multiple_of(c * R, R)
            at = pl.ds(base, R)
            live = live_of(base, R)
            total = jnp.zeros((R, 128), f32)
            for r in range(8):
                window = gat[h, pl.ds(base + r, R + 24), :]
                for j in range(4):
                    total = total + taps_ref[pl.ds(r + 8 * j, 1), cols] * window[8 * j : 8 * j + R]
            sg = jax.nn.sigmoid(total)
            act[at, cols] = (total * sg * live).astype(bf)
            d = dact[at, cols] * live * sg * (1.0 + total * (1.0 - sg))
            dfl[h, pl.ds(base + 16, R), :] = d
            for r in range(8):
                window = gat[h, pl.ds(base + r, R + 24), :]
                for j in range(4):
                    prod = d * window[8 * j : 8 * j + R]
                    k = r + 8 * j
                    kacc[k] = kacc[k] + jnp.sum(prod.reshape(R // 8, 8, 128), axis=0)
            return carry

        lax.fori_loop(0, 512 // R, forward, 0)
        kall[i * 2 + h] = jnp.sum(kacc[...], axis=1)

        def backward(c, carry):
            base = pl.multiple_of(c * R, R)
            at = pl.ds(base, R)
            live = live_of(base, R)
            total = jnp.zeros((R, 128), f32)
            for r in range(8):
                first = r if r else 8
                window = dfl[h, pl.ds(base + first, R + 24), :]
                for j in range(4):
                    total = total + taps_ref[pl.ds(32 - first - 8 * j, 1), cols] * window[8 * j : 8 * j + R]
            total = total * live
            sg, v = gsig[at, cols], vals[at, cols]
            dpv[at, cols] = (total * sg).astype(bf)
            dpg[at, cols] = (total * v * sg * (1.0 - sg)).astype(bf)
            return carry

        lax.fori_loop(0, 512 // R, backward, 0)

    def pack(part, start, tiles_wide, column):
        for h in range(2):
            for s in range(8):
                for rt in range(6):
                    at = start + (rt * tiles_wide + column + h) * 16
                    row = s * 96 + rt * 16
                    g_ref[s, pl.ds(pl.multiple_of(at, 16), 16), :] = part[row : row + 16, h * 128 : h * 128 + 128]

    pack(dot(cot_t[...], act[...], NN).astype(bf), 1152, 6, i * 2)
    pack(dot(scaled_t[...], dpv[...], NN).astype(bf), 0, 12, i * 2)
    pack(dot(scaled_t[...], dpg[...], NN).astype(bf), 0, 12, 6 + i * 2)
    m = dot(act[...], dt_ref[...], NT)
    d = dot(dpv[...], upv_ref[...], NT) + dot(dpg[...], upg_ref[...], NT)

    @pl.when(i == 0)
    def _():
        mixed[...] = m
        dsc[...] = d

    @pl.when(i > 0)
    def _():
        mixed[...] += m
        dsc[...] += d

    @pl.when(i == 2)
    def _():
        gain = gain_ref[...]

        def finish(c, gsum):
            at = pl.ds(pl.multiple_of(c * 32, 32), 32)
            res_ref[at, :] = (x_ref[at, :].astype(f32) + mixed[at, :]).astype(bf)
            ds, n = dsc[at, :], normed[at, :]
            prod = ds * n
            dn = ds * gain
            inv = invs[at, :][:, :1]
            grad = inv * (dn - jnp.mean(dn, axis=1, keepdims=True)
                          - n * jnp.mean(prod * gain, axis=1, keepdims=True))
            gin_ref[at, :] = (ct_ref[at, :].astype(f32) + grad).astype(bf)
            return gsum + jnp.sum(prod.reshape(4, 8, 768), axis=0)

        gsum = lax.fori_loop(0, 16, finish, jnp.zeros((8, 768), f32))
        gsum = jnp.sum(gsum, axis=0, keepdims=True)
        small = jnp.concatenate([kall[b] for b in range(6)], axis=1)
        small = jnp.concatenate([small, jnp.broadcast_to(gsum, (16, 768))], axis=0)
        for s in range(8):
            g_ref[s, pl.ds(1728, 48), pl.ds(0, 96)] = small[:, s * 96 : s * 96 + 96].astype(bf)


def layer(lengths, frames, cot, full, taps, gain):
    f32, bf = jnp.float32, jnp.bfloat16
    whole = lambda r, c: pl.BlockSpec((r, c), lambda i: (0, 0))
    return pl.pallas_call(
        layer_kernel,
        grid=(3,),
        out_shape=(
            jax.ShapeDtypeStruct((512, 768), bf),
            jax.ShapeDtypeStruct((512, 768), bf),
            jax.ShapeDtypeStruct((8, 1792, 128), bf),
        ),
        in_specs=[
            pl.BlockSpec(memory_space=pltpu.SMEM),
            whole(512, 768),
            whole(512, 768),
            pl.BlockSpec((768, 256), lambda i: (0, i)),
            pl.BlockSpec((768, 256), lambda i: (0, 3 + i)),
            pl.BlockSpec((768, 256), lambda i: (0, 6 + i)),
            pl.BlockSpec((32, 256), lambda i: (0, i)),
            whole(1, 768),
        ],
        out_specs=(
            whole(512, 768),
            whole(512, 768),
            pl.BlockSpec((8, 1792, 128), lambda i: (0, 0, 0)),
        ),
        scratch_shapes=[
            pltpu.VMEM((512, 768), f32),
            pltpu.VMEM((512, 128), f32),
            pltpu.VMEM((512, 768), bf),
            pltpu.VMEM((768, 512), bf),
            pltpu.VMEM((768, 512), bf),
            pltpu.VMEM((512, 256), f32),
            pltpu.VMEM((512, 256), f32),
            pltpu.VMEM((512, 256), f32),
            pltpu.VMEM((2, 544, 128), f32),
            pltpu.VMEM((2, 544, 128), f32),
            pltpu.VMEM((512, 256), bf),
            pltpu.VMEM((512, 256), bf),
            pltpu.VMEM((512, 256), bf),
            pltpu.VMEM((512, 768), f32),
            pltpu.VMEM((512, 768), f32),
            pltpu.VMEM((32, 8, 128), f32),
            pltpu.VMEM((6, 32, 128), f32),
        ],
        compiler_params=pltpu.CompilerParams(vmem_limit_bytes=48 * 1024 * 1024),
        name="layer",
    )(lengths, frames, cot, full, full, full, taps, gain)


def body(frames_in, lengths, up_weight, norm_gain, conv_kernel, down_weight, cotangent):
    bf = jnp.bfloat16
    small = jnp.pad(jnp.concatenate([conv_kernel, norm_gain[None, :]], axis=0), ((0, 63), (0, 32)))
    packed = jnp.concatenate([up_weight, down_weight.T, small], axis=1)
    full = gather_weights(packed)
    small = full[:, 2304:].reshape(8, 96, 128)[:, :33, :96].transpose(1, 0, 2).reshape(33, 768)
    small = small.astype(jnp.float32)
    result, grad_in, parts = layer(
        lengths, frames_in.reshape(512, 768), cotangent.reshape(512, 768), full, small[:32], small[32:]
    )
    factor = 1.0 / 262144.0 ** 0.5
    up_total, down_total, rest = reduce_parts(parts.reshape(4, 2, 2, 896, 128), factor)
    return (
        result.reshape(1, 512, 768),
        grad_in.reshape(1, 512, 768),
        up_total,
        rest[32, :96],
        rest[:32, :96],
        down_total.T,
    )


def solution(mesh):
    return jax.shard_map(
        body,
        mesh=mesh,
        in_specs=(
            P(("replica", "shard"), None, None),
            P(("replica", "shard")),
            P("shard", None),
            P("shard"),
            P(None, "shard"),
            P(None, "shard"),
            P(("replica", "shard"), None, None),
        ),
        out_specs=(
            P(("replica", "shard"), None, None),
            P(("replica", "shard"), None, None),
            P("shard", None),
            P("shard"),
            P(None, "shard"),
            P(None, "shard"),
        ),
        check_vma=False,
    )
```

```python
import functools

import jax
import jax.numpy as jnp
from jax import lax
from jax.experimental import pallas as pl
from jax.experimental.pallas import tpu as pltpu
from jax.sharding import PartitionSpec as P

EPS = 1e-05
WIDE = 2432
CUT = 1280
MESH = pl.DeviceIdType.MESH


def place():
    rep, sh = lax.axis_index("replica"), lax.axis_index("shard")
    z, y_hi, core = rep // 4, (rep // 2) % 2, rep % 2
    x, y_lo = sh // 2, sh % 2
    return x, y_hi * 2 + y_lo, z, core


def device(x, y, z, core):
    return ((z * 2 + y // 2) * 2 + core, x * 2 + y % 2)


def greet(partners):
    barrier = pltpu.get_barrier_semaphore()
    for partner in partners:
        pl.semaphore_signal(barrier, inc=1, device_id=partner, device_id_type=MESH)
    pl.semaphore_wait(barrier, len(partners))


def gather_kernel(w_ref, out_ref, local_sem, send_sem, recv_sem):
    x, y, z, core = place()
    y_lo = y % 2
    xp, xm, x2 = (x + 1) % 4, (x + 3) % 4, (x + 2) % 4
    yp, ym = (y + 1) % 4, (y + 3) % 4
    to_xp, to_xm = device(xp, y, z, core), device(xm, y, z, core)
    to_yp, to_ym = device(x, yp, z, core), device(x, ym, z, core)
    to_sib = device(x, y, z, 1 - core)
    greet([to_xp, to_xm, to_yp, to_ym, to_sib])

    def rows(bx, byl):
        return pl.ds(pl.multiple_of((bx * 2 + byl) * 96 + core * 48, 16), 48)

    LO, HI, ALL = pl.ds(0, CUT), pl.ds(CUT, WIDE - CUT), pl.ds(0, WIDE)
    own = pl.multiple_of((x * 2 + y_lo) * 96, 16)
    local = pltpu.make_async_copy(w_ref, out_ref.at[pl.ds(own, 96)], local_sem)
    local.start()
    mine = pl.ds(pl.multiple_of(core * 48, 16), 48)
    sent = []

    def send(index, bx, byl, cols, target, own_block=False):
        dst = out_ref.at[rows(bx, byl), cols]
        src = w_ref.at[mine, cols] if own_block else dst
        copy = pltpu.make_async_remote_copy(
            src_ref=src, dst_ref=dst, send_sem=send_sem.at[index], recv_sem=recv_sem.at[index],
            device_id=target, device_id_type=MESH)
        copy.start()
        sent.append(copy)

    def arrive(index, bx, byl, cols):
        dst = out_ref.at[rows(bx, byl), cols]
        pltpu.make_async_remote_copy(
            src_ref=dst, dst_ref=dst, send_sem=send_sem.at[index], recv_sem=recv_sem.at[index],
            device_id=to_sib, device_id_type=MESH).wait_recv()

    oth = 1 - y_lo
    send(0, x, y_lo, ALL, to_xp, True)
    send(1, x, y_lo, ALL, to_xm, True)
    send(4, x, y_lo, LO, to_yp, True)
    send(8, x, y_lo, HI, to_ym, True)
    arrive(0, xm, y_lo, ALL)
    send(2, xm, y_lo, LO, to_xp)
    send(5, xm, y_lo, LO, to_yp)
    send(9, xm, y_lo, HI, to_ym)
    arrive(1, xp, y_lo, ALL)
    send(3, xp, y_lo, HI, to_xm)
    send(6, xp, y_lo, LO, to_yp)
    send(10, xp, y_lo, HI, to_ym)
    send(12, xm, y_lo, ALL, to_sib)
    send(13, xp, y_lo, ALL, to_sib)
    arrive(4, x, oth, LO)
    send(16, x, oth, LO, to_sib)
    arrive(8, x, oth, HI)
    send(20, x, oth, HI, to_sib)
    arrive(2, x2, y_lo, LO)
    send(7, x2, y_lo, LO, to_yp)
    send(14, x2, y_lo, LO, to_sib)
    arrive(3, x2, y_lo, HI)
    send(11, x2, y_lo, HI, to_ym)
    send(15, x2, y_lo, HI, to_sib)
    for k, bx in ((1, xm), (2, xp), (3, x2)):
        arrive(4 + k, bx, oth, LO)
        send(16 + k, bx, oth, LO, to_sib)
        arrive(8 + k, bx, oth, HI)
        send(20 + k, bx, oth, HI, to_sib)

    def sib_rows(bx, byl):
        return pl.ds(pl.multiple_of((bx * 2 + byl) * 96 + (1 - core) * 48, 16), 48)

    def arrive_sib(index, bx, byl, cols):
        dst = out_ref.at[sib_rows(bx, byl), cols]
        pltpu.make_async_remote_copy(
            src_ref=dst, dst_ref=dst, send_sem=send_sem.at[index], recv_sem=recv_sem.at[index],
            device_id=to_sib, device_id_type=MESH).wait_recv()

    arrive_sib(12, xm, y_lo, ALL)
    arrive_sib(13, xp, y_lo, ALL)
    arrive_sib(14, x2, y_lo, LO)
    arrive_sib(15, x2, y_lo, HI)
    for k, bx in ((0, x), (1, xm), (2, xp), (3, x2)):
        arrive_sib(16 + k, bx, oth, LO)
        arrive_sib(20 + k, bx, oth, HI)
    for copy in sent:
        copy.wait_send()
    local.wait()


def gather_weights(packed):
    return pl.pallas_call(
        gather_kernel,
        out_shape=jax.ShapeDtypeStruct((768, WIDE), jnp.bfloat16),
        in_specs=[pl.BlockSpec(memory_space=pltpu.VMEM)],
        out_specs=pl.BlockSpec(memory_space=pltpu.VMEM),
        scratch_shapes=[
            pltpu.SemaphoreType.DMA,
            pltpu.SemaphoreType.DMA((24,)),
            pltpu.SemaphoreType.DMA((24,)),
        ],
        compiler_params=pltpu.CompilerParams(collective_id=0, has_side_effects=True),
        name="gather_weights",
    )(packed)


def add_rows(rows, step, dst, terms):
    def one(i, carry):
        at = pl.ds(pl.multiple_of(i * step, 16), step)
        total = terms[0](at).astype(jnp.float32)
        for term in terms[1:]:
            total = total + term(at).astype(jnp.float32)
        dst(at, total)
        return carry

    lax.fori_loop(0, rows // step, one, 0)


ROWS, START = (288, 288, 320), (0, 288, 576)


def layer_kernel(factor, len_ref, x_ref, ct_ref, w_ref, taps_ref, gain_ref,
                 res_ref, gin_ref, up_ref, down_ref, rest_ref,
                 normed, invs, scaled, scaled_t, cot_t, vals, gsig, dact, gat, dfl, act, dpv, dpg,
                 mixed, dsc, kacc, kall,
                 g, cr, cs, xr, xq, xs, yr, yq, zs, zr, fin,
                 send_sem, recv_sem, zsend, zrecv, asend, arecv):
    f32, bf = jnp.float32, jnp.bfloat16
    length = len_ref[0]
    x, y, z, core = place()
    y_lo, y_hi = y % 2, y // 2
    xp, xm, x2 = (x + 1) % 4, (x + 3) % 4, (x + 2) % 4
    yp, ym, y2 = (y + 1) % 4, (y + 3) % 4, (y + 2) % 4
    to_xp, to_xm = device(xp, y, z, core), device(xm, y, z, core)
    to_yp, to_ym = device(x, yp, z, core), device(x, ym, z, core)
    to_y2 = device(x, y2, z, core)
    to_sib = device(x, y, z, 1 - core)

    barrier = pltpu.get_barrier_semaphore()
    for partner in (to_xp, to_xm, to_yp, to_ym, to_y2, to_sib):
        pl.semaphore_signal(barrier, inc=1, device_id=partner, device_id_type=MESH)

    def hello(d, carry):
        pl.semaphore_signal(barrier, inc=1, device_id=device(x, y, (z + d) % 16, core), device_id_type=MESH)
        return carry

    lax.fori_loop(1, 16, hello, 0)
    sent = []

    def copy(index, src, dst, target):
        return pltpu.make_async_remote_copy(
            src_ref=src, dst_ref=dst, send_sem=send_sem.at[index], recv_sem=recv_sem.at[index],
            device_id=target, device_id_type=MESH)

    def send(index, src, dst, target):
        c = copy(index, src, dst, target)
        c.start()
        sent.append(c)

    def arrive(index, dst):
        copy(index, dst, dst, to_sib).wait_recv()


    def live_of(base, rows):
        return ((lax.broadcasted_iota(jnp.int32, (rows, 128), 0) + base) < length).astype(f32)


    gain = gain_ref[...]

    def norm(c, carry):
        at = pl.ds(pl.multiple_of(c * 32, 32), 32)
        v = x_ref[at, :].astype(f32)
        centred = v - jnp.mean(v, axis=1, keepdims=True)
        inv = lax.rsqrt(jnp.mean(centred * centred, axis=1, keepdims=True) + EPS)
        n = centred * inv
        normed[at, :] = n
        invs[at, :] = jnp.broadcast_to(inv, (32, 128))
        scaled[at, :] = (n * gain).astype(bf)
        return carry

    lax.fori_loop(0, 16, norm, 0)
    scaled_t[...] = scaled[...].T
    cot_t[...] = ct_ref[...].T
    for buf in (gat, dfl):
        for h in range(2):
            buf[h, pl.ds(0, 16), :] = jnp.zeros((16, 128), f32)
            buf[h, pl.ds(528, 16), :] = jnp.zeros((16, 128), f32)
    for s in range(8):
        g[2, s // 2, s % 2, 1, pl.ds(256, 64), :] = jnp.zeros((64, 128), bf)


    dot = functools.partial(lax.dot_general, preferred_element_type=f32)
    NN, NT = (((1,), (0,)), ((), ())), (((1,), (1,)), ((), ()))


    order = (x2, xp, xm, x)

    def core_start(b):
        n = pl.ds(0, ROWS[b])
        for k, bx in enumerate(order):
            send(b * 10 + k, g.at[b, bx, :, 1 - core, n], cr.at[b, bx, :, n], to_sib)

    def core_sum(b, k):
        bx, n = order[k], ROWS[b]
        arrive(b * 10 + k, cr.at[b, bx, :, pl.ds(0, n)])
        for j in range(2):
            def put(at, v):
                cs[b, bx, j, at, :] = v.astype(bf)
            add_rows(n, n // 4 if n == 320 else n // 3, put,
                     [lambda at: g[b, bx, j, core, at, :], lambda at: cr[b, bx, j, at, :]])

    def x_first(b):
        n, at = b * 10, pl.ds(0, ROWS[b])
        core_sum(b, 0)
        send(n + 4, cs.at[b, x2, 0, at], xq.at[b, 0, at], to_xp)
        send(n + 5, cs.at[b, x2, 1, at], xq.at[b, 1, at], to_xm)
        core_sum(b, 1)
        send(n + 6, cs.at[b, xp, 1, at], xr.at[b, 0, 1, at], to_xp)
        core_sum(b, 2)
        send(n + 7, cs.at[b, xm, 0, at], xr.at[b, 1, 0, at], to_xm)
        core_sum(b, 3)

    def x_second(b):
        n, rows = b * 10, pl.ds(0, ROWS[b])
        step = ROWS[b] // 4 if ROWS[b] == 320 else ROWS[b] // 3
        for q, bx, target in ((0, xp, to_xp), (1, xm, to_xm)):
            arrive(n + 4 + q, xq.at[b, q, rows])

            def put(at, v):
                cs[b, bx, q, at, :] = v.astype(bf)

            add_rows(ROWS[b], step, put, [lambda at: cs[b, bx, q, at, :], lambda at: xq[b, q, at, :]])
            send(n + 8 + q, cs.at[b, bx, q, rows], xr.at[b, q, q, rows], target)

    def x_last(b):
        n, rows = b * 10, pl.ds(0, ROWS[b])
        step = ROWS[b] // 4 if ROWS[b] == 320 else ROWS[b] // 3
        arrive(n + 6, xr.at[b, 0, 1, rows])
        arrive(n + 7, xr.at[b, 1, 0, rows])
        arrive(n + 8, xr.at[b, 0, 0, rows])
        arrive(n + 9, xr.at[b, 1, 1, rows])
        for j in range(2):
            def put(at, v):
                xs[j, pl.ds(pl.multiple_of(START[b] + at.start, 16), step), :] = v.astype(bf)
            add_rows(ROWS[b], step, put, [lambda at: cs[b, x, j, at, :], lambda at: xr[b, 0, j, at, :],
                                          lambda at: xr[b, 1, j, at, :]])

    def pack(b, part, kind):
        for h in range(2):
            for s in range(8):
                for rt in range(6):
                    t = kind * 12 + rt * 2 + h
                    per, row = ROWS[b] // 16, s * 96 + rt * 16
                    g[b, s // 2, s % 2, t // per, pl.ds(t % per * 16, 16), :] = part[
                        row : row + 16, h * 128 : h * 128 + 128]

    R = 64
    for b in range(3):
        v_cols, g_cols, d_cols = pl.ds(b * 256, 256), pl.ds(768 + b * 256, 256), pl.ds(1536 + b * 256, 256)
        def gate(c, carry):
            base = pl.multiple_of(c * 128, 128)
            at = pl.ds(base, 128)
            live = live_of(base, 128)
            v = dot(scaled[at, :], w_ref[:, v_cols], NN)
            sg = jax.nn.sigmoid(dot(scaled[at, :], w_ref[:, g_cols], NN))
            vals[at, :] = v
            gsig[at, :] = sg
            dact[at, :] = dot(ct_ref[at, :], w_ref[:, d_cols], NN)
            for h in range(2):
                cols = slice(h * 128, h * 128 + 128)
                gat[h, pl.ds(base + 16, 128), :] = (v[:, cols] * sg[:, cols] * live).astype(bf).astype(f32)
            return carry

        lax.fori_loop(0, 4, gate, 0)

        for h in range(2):
            cols = pl.ds(h * 128, 128)
            taps_cols = pl.ds(b * 256 + h * 128, 128)
            kacc[...] = jnp.zeros_like(kacc)

            def forward(c, carry):
                base = pl.multiple_of(c * R, R)
                at = pl.ds(base, R)
                live = live_of(base, R)
                total = jnp.zeros((R, 128), f32)
                for r in range(8):
                    window = gat[h, pl.ds(base + r, R + 24), :]
                    for j in range(4):
                        total = total + taps_ref[pl.ds(r + 8 * j, 1), taps_cols] * window[8 * j : 8 * j + R]
                sg = jax.nn.sigmoid(total)
                act[at, cols] = (total * sg * live).astype(bf)
                d = dact[at, cols] * live * sg * (1.0 + total * (1.0 - sg))
                dfl[h, pl.ds(base + 16, R), :] = d
                for r in range(8):
                    window = gat[h, pl.ds(base + r, R + 24), :]
                    for j in range(4):
                        prod = d * window[8 * j : 8 * j + R]
                        k = r + 8 * j
                        kacc[k] = kacc[k] + jnp.sum(prod.reshape(R // 8, 8, 128), axis=0)
                return carry

            lax.fori_loop(0, 512 // R, forward, 0)
            kall[b * 2 + h] = jnp.sum(kacc[...], axis=1)

            def backward(c, carry):
                base = pl.multiple_of(c * R, R)
                at = pl.ds(base, R)
                live = live_of(base, R)
                total = jnp.zeros((R, 128), f32)
                for r in range(8):
                    first = r if r else 8
                    window = dfl[h, pl.ds(base + first, R + 24), :]
                    for j in range(4):
                        total = total + taps_ref[pl.ds(32 - first - 8 * j, 1), taps_cols] * window[8 * j : 8 * j + R]
                total = total * live
                sg, v = gsig[at, cols], vals[at, cols]
                dpv[at, cols] = (total * sg).astype(bf)
                dpg[at, cols] = (total * v * sg * (1.0 - sg)).astype(bf)
                return carry

            lax.fori_loop(0, 512 // R, backward, 0)


            if b and not h:
                x_first(b - 1)
                if b == 2:
                    x_last(0)
        if b:
            x_second(b - 1)
        pack(b, dot(scaled_t[...], dpv[...], NN).astype(bf), 0)
        pack(b, dot(scaled_t[...], dpg[...], NN).astype(bf), 1)
        pack(b, dot(cot_t[...], act[...], NN).astype(bf), 2)
        if b == 0:
            pl.semaphore_wait(barrier, 21)
        if b < 2:
            core_start(b)
        m = dot(act[...], w_ref[:, d_cols], NT)
        d = dot(dpv[...], w_ref[:, v_cols], NT) + dot(dpg[...], w_ref[:, g_cols], NT)
        if b:
            mixed[...] += m
            dsc[...] += d
        else:
            mixed[...] = m
            dsc[...] = d

    def finish(c, gsum):
        at = pl.ds(pl.multiple_of(c * 32, 32), 32)
        ds, n = dsc[at, :], normed[at, :]
        prod = ds * n
        dn = ds * gain
        inv = invs[at, :][:, :1]
        grad = inv * (dn - jnp.mean(dn, axis=1, keepdims=True)
                      - n * jnp.mean(prod * gain, axis=1, keepdims=True))
        gin_ref[at, :] = (ct_ref[at, :].astype(f32) + grad).astype(bf)
        return gsum + jnp.sum(prod.reshape(4, 8, 768), axis=0)

    gsum = lax.fori_loop(0, 16, finish, jnp.zeros((8, 768), f32))
    gsum = jnp.sum(gsum, axis=0, keepdims=True)
    small = jnp.concatenate([kall[b] for b in range(6)], axis=1)
    small = jnp.concatenate([small, jnp.broadcast_to(gsum, (16, 768))], axis=0)
    for s in range(8):
        g[2, s // 2, s % 2, 1, pl.ds(256, 48), pl.ds(0, 96)] = small[:, s * 96 : s * 96 + 96].astype(bf)
    core_start(2)
    x_last(1)
    x_first(2)
    x_second(2)
    x_last(2)
    def part(yy, half, rows=224):
        return xs.at[yy % 2, pl.ds(pl.multiple_of((yy // 2) * 448 + half * 224, 16), rows)]

    send(30, part(y2, 0), yq.at[0], to_yp)
    send(31, part(y2, 1), yq.at[1], to_ym)
    send(32, part(yp, 1), yr.at[0, 1], to_yp)
    send(33, part(ym, 0), yr.at[1, 0], to_ym)
    arrive(30, yq.at[0])
    dst_p = part(yp, 0)

    def put_yp(at, v):
        dst_p[at, :] = v.astype(jnp.bfloat16)

    add_rows(224, 32, put_yp, [lambda at: dst_p[at, :], lambda at: yq[0, at, :]])
    send(34, part(yp, 0), yr.at[0, 0], to_yp)
    arrive(31, yq.at[1])
    dst_m = part(ym, 1)

    def put_ym(at, v):
        dst_m[at, :] = v.astype(jnp.bfloat16)

    add_rows(224, 32, put_ym, [lambda at: dst_m[at, :], lambda at: yq[1, at, :]])
    send(35, part(ym, 1), yr.at[1, 1], to_ym)
    arrive(32, yr.at[0, 1])
    arrive(33, yr.at[1, 0])
    arrive(34, yr.at[0, 0])
    arrive(35, yr.at[1, 1])
    zs[pl.ds(448, 64), :] = jnp.zeros((64, 128), jnp.bfloat16)
    for half in range(2):
        mine = part(y, half)

        def put(at, v):
            zs[pl.ds(pl.multiple_of(half * 224 + at.start, 16), 32), :] = v.astype(jnp.bfloat16)

        add_rows(224, 32, put, [lambda at: mine[at, :], lambda at: yr[0, half, at, :], lambda at: yr[1, half, at, :]])


    def piece(p):
        return pl.ds(pl.multiple_of(p * 32, 32), 32)

    def z_copy(d):
        to = (z + d) % 16
        return pltpu.make_async_remote_copy(
            src_ref=zs.at[piece(to)], dst_ref=zr.at[d], send_sem=zsend.at[d], recv_sem=zrecv.at[d],
            device_id=device(x, y, to, core), device_id_type=MESH)

    def z_start(d, carry):
        z_copy(d).start()
        return carry

    lax.fori_loop(1, 16, z_start, 0)

    def residual(c, carry):
        at = pl.ds(pl.multiple_of(c * 64, 64), 64)
        res_ref[at, :] = (x_ref[at, :].astype(f32) + mixed[at, :]).astype(bf)
        return carry

    lax.fori_loop(0, 8, residual, 0)

    def z_add(d, total):
        z_copy(d).wait_recv()
        return total + zr[d].astype(jnp.float32)

    total = lax.fori_loop(1, 16, z_add, zs[piece(z), :].astype(jnp.float32))
    mine_at = fin.at[core, y_hi]
    mine_at[piece(z), :] = total.astype(jnp.bfloat16)

    def a_copy(d, p):
        at = fin.at[core, y_hi, piece(p)]
        return pltpu.make_async_remote_copy(
            src_ref=at, dst_ref=at, send_sem=asend.at[d], recv_sem=arecv.at[d],
            device_id=device(x, y, (z + d) % 16, core), device_id_type=MESH)

    def a_start(d, carry):
        a_copy(d, z).start()
        return carry

    lax.fori_loop(1, 16, a_start, 0)

    def a_wait(d, carry):
        a_copy(d, (z + 16 - d) % 16).wait_recv()
        return carry

    lax.fori_loop(1, 16, a_wait, 0)
    both = fin.at[core, y_hi, pl.ds(0, 448)]
    send(36, both, both, to_y2)
    send(37, both, both, to_sib)
    far = fin.at[core, 1 - y_hi, pl.ds(0, 448)]
    arrive(36, far)
    send(38, far, far, to_sib)

    def z_done(d, carry):
        z_copy(d).wait_send()
        a_copy(d, z).wait_send()
        return carry

    lax.fori_loop(1, 16, z_done, 0)
    arrive(37, fin.at[1 - core, y_hi, pl.ds(0, 448)])
    arrive(38, fin.at[1 - core, 1 - y_hi, pl.ds(0, 448)])

    def tile(b, t):
        per = ROWS[b] // 16
        row = START[b] + t % per * 16
        return fin[t // per, row // 448, pl.ds(row % 448, 16), :].astype(f32) * factor

    for b in range(3):
        for h in range(2):
            at = (b * 2 + h) * 128
            for rt in range(6):
                rows = pl.ds(rt * 16, 16)
                up_ref[rows, pl.ds(at, 128)] = tile(b, rt * 2 + h)
                up_ref[rows, pl.ds(768 + at, 128)] = tile(b, 12 + rt * 2 + h)
                down_ref[rows, pl.ds(at, 128)] = tile(b, 24 + rt * 2 + h)
    for k in range(3):
        rest_ref[pl.ds(k * 16, 16), :] = tile(2, 36 + k)
    for c in sent:
        c.wait_send()


def layer(lengths, frames, cot, full, taps, gain, factor):
    f32, bf = jnp.float32, jnp.bfloat16
    vmem = pl.BlockSpec(memory_space=pltpu.VMEM)
    return pl.pallas_call(
        functools.partial(layer_kernel, factor),
        out_shape=(
            jax.ShapeDtypeStruct((512, 768), bf),
            jax.ShapeDtypeStruct((512, 768), bf),
            jax.ShapeDtypeStruct((96, 1536), f32),
            jax.ShapeDtypeStruct((96, 768), f32),
            jax.ShapeDtypeStruct((48, 128), f32),
        ),
        in_specs=[pl.BlockSpec(memory_space=pltpu.SMEM)] + [vmem] * 5,
        out_specs=(vmem,) * 5,
        scratch_shapes=[
            pltpu.VMEM((512, 768), f32),
            pltpu.VMEM((512, 128), f32),
            pltpu.VMEM((512, 768), bf),
            pltpu.VMEM((768, 512), bf),
            pltpu.VMEM((768, 512), bf),
            pltpu.VMEM((512, 256), f32),
            pltpu.VMEM((512, 256), f32),
            pltpu.VMEM((512, 256), f32),
            pltpu.VMEM((2, 544, 128), f32),
            pltpu.VMEM((2, 544, 128), f32),
            pltpu.VMEM((512, 256), bf),
            pltpu.VMEM((512, 256), bf),
            pltpu.VMEM((512, 256), bf),
            pltpu.VMEM((512, 768), f32),
            pltpu.VMEM((512, 768), f32),
            pltpu.VMEM((32, 8, 128), f32),
            pltpu.VMEM((6, 32, 128), f32),
            pltpu.VMEM((3, 4, 2, 2, 320, 128), bf),
            pltpu.VMEM((3, 4, 2, 320, 128), bf),
            pltpu.VMEM((3, 4, 2, 320, 128), bf),
            pltpu.VMEM((3, 2, 2, 320, 128), bf),
            pltpu.VMEM((3, 2, 320, 128), bf),
            pltpu.VMEM((2, 896, 128), bf),
            pltpu.VMEM((2, 2, 224, 128), bf),
            pltpu.VMEM((2, 224, 128), bf),
            pltpu.VMEM((512, 128), bf),
            pltpu.VMEM((16, 32, 128), bf),
            pltpu.VMEM((2, 2, 512, 128), bf),
            pltpu.SemaphoreType.DMA((39,)),
            pltpu.SemaphoreType.DMA((39,)),
            pltpu.SemaphoreType.DMA((16,)),
            pltpu.SemaphoreType.DMA((16,)),
            pltpu.SemaphoreType.DMA((16,)),
            pltpu.SemaphoreType.DMA((16,)),
        ],
        compiler_params=pltpu.CompilerParams(
            collective_id=1, has_side_effects=True, vmem_limit_bytes=48 * 1024 * 1024),
        name="layer",
    )(lengths, frames, cot, full, taps, gain)


def body(frames_in, lengths, up_weight, norm_gain, conv_kernel, down_weight, cotangent):
    bf = jnp.bfloat16
    small = jnp.pad(jnp.concatenate([conv_kernel, norm_gain[None, :]], axis=0), ((0, 63), (0, 32)))
    packed = jnp.concatenate([up_weight, down_weight.T, small], axis=1)
    full = gather_weights(packed)
    small = full[:, 2304:].reshape(8, 96, 128)[:, :33, :96].transpose(1, 0, 2).reshape(33, 768)
    small = small.astype(jnp.float32)
    factor = 1.0 / 262144.0 ** 0.5
    result, grad_in, up_total, down_total, rest = layer(
        lengths, frames_in.reshape(512, 768), cotangent.reshape(512, 768), full, small[:32], small[32:], factor
    )
    return (
        result.reshape(1, 512, 768),
        grad_in.reshape(1, 512, 768),
        up_total,
        rest[32, :96],
        rest[:32, :96],
        down_total.T,
    )


def solution(mesh):
    return jax.shard_map(
        body,
        mesh=mesh,
        in_specs=(
            P(("replica", "shard"), None, None),
            P(("replica", "shard")),
            P("shard", None),
            P("shard"),
            P(None, "shard"),
            P(None, "shard"),
            P(("replica", "shard"), None, None),
        ),
        out_specs=(
            P(("replica", "shard"), None, None),
            P(("replica", "shard"), None, None),
            P("shard", None),
            P("shard"),
            P(None, "shard"),
            P(None, "shard"),
        ),
        check_vma=False,
    )
```

```python
import functools

import jax
import jax.numpy as jnp
from jax import lax
from jax.experimental import pallas as pl
from jax.experimental.pallas import tpu as pltpu
from jax.sharding import PartitionSpec as P

EPS = 1e-05
WIDE = 896
CUT = 512
MESH = pl.DeviceIdType.MESH


def place():
    rep, sh = lax.axis_index("replica"), lax.axis_index("shard")
    z, y_hi, core = rep // 4, (rep // 2) % 2, rep % 2
    x, y_lo = sh // 2, sh % 2
    return x, y_hi * 2 + y_lo, z, core


def device(x, y, z, core):
    return ((z * 2 + y // 2) * 2 + core, x * 2 + y % 2)


def greet(partners):
    barrier = pltpu.get_barrier_semaphore()
    for partner in partners:
        pl.semaphore_signal(barrier, inc=1, device_id=partner, device_id_type=MESH)
    pl.semaphore_wait(barrier, len(partners))


def gather_steps(own_ref, first, out_ref, width, cut, local_sem, send_sem, recv_sem, base):
    x, y, z, core = place()
    y_lo = y % 2
    xp, xm, x2 = (x + 1) % 4, (x + 3) % 4, (x + 2) % 4
    yp, ym = (y + 1) % 4, (y + 3) % 4
    to_xp, to_xm = device(xp, y, z, core), device(xm, y, z, core)
    to_yp, to_ym = device(x, yp, z, core), device(x, ym, z, core)
    to_sib = device(x, y, z, 1 - core)
    oth = 1 - y_lo
    LO, HI, ALL = (0, cut), (cut, width - cut), (0, width)
    mine = pl.ds(pl.multiple_of(core * 48, 16), 48)
    local = pltpu.make_async_copy(
        own_ref.at[:, pl.ds(first, width)],
        out_ref.at[pl.ds(pl.multiple_of((x * 2 + y_lo) * 96, 16), 96)], local_sem)
    sent = []

    def block(bx, byl, cols, who):
        return out_ref.at[pl.ds(pl.multiple_of((bx * 2 + byl) * 96 + who * 48, 16), 48), pl.ds(*cols)]

    def copy(index, src, dst, target):
        return pltpu.make_async_remote_copy(
            src_ref=src, dst_ref=dst, send_sem=send_sem.at[base + index], recv_sem=recv_sem.at[base + index],
            device_id=target, device_id_type=MESH)

    def send(index, bx, byl, cols, target, own=False):
        dst = block(bx, byl, cols, core)
        src = own_ref.at[mine, pl.ds(first + cols[0], cols[1])] if own else dst
        c = copy(index, src, dst, target)
        c.start()
        sent.append(c)

    def arrive(index, bx, byl, cols, who):
        dst = block(bx, byl, cols, who)
        copy(index, dst, dst, to_sib).wait_recv()

    def begin():
        local.start()
        send(0, x, y_lo, ALL, to_xp, True)
        send(1, x, y_lo, ALL, to_xm, True)
        send(4, x, y_lo, LO, to_yp, True)
        send(8, x, y_lo, HI, to_ym, True)

    def across(k, bx):
        arrive(4 + k, bx, oth, LO, core)
        send(16 + k, bx, oth, LO, to_sib)
        arrive(8 + k, bx, oth, HI, core)
        send(20 + k, bx, oth, HI, to_sib)

    def second():
        arrive(0, xm, y_lo, ALL, core)
        send(2, xm, y_lo, LO, to_xp)
        send(5, xm, y_lo, LO, to_yp)
        send(9, xm, y_lo, HI, to_ym)
        arrive(1, xp, y_lo, ALL, core)
        send(3, xp, y_lo, HI, to_xm)
        send(6, xp, y_lo, LO, to_yp)
        send(10, xp, y_lo, HI, to_ym)
        send(12, xm, y_lo, ALL, to_sib)
        send(13, xp, y_lo, ALL, to_sib)
        across(0, x)

    def third():
        arrive(2, x2, y_lo, LO, core)
        send(7, x2, y_lo, LO, to_yp)
        send(14, x2, y_lo, LO, to_sib)
        arrive(3, x2, y_lo, HI, core)
        send(11, x2, y_lo, HI, to_ym)
        send(15, x2, y_lo, HI, to_sib)
        across(1, xm)
        across(2, xp)

    def fourth():
        across(3, x2)

    def last():
        sib = 1 - core
        arrive(12, xm, y_lo, ALL, sib)
        arrive(13, xp, y_lo, ALL, sib)
        arrive(14, x2, y_lo, LO, sib)
        arrive(15, x2, y_lo, HI, sib)
        for k, bx in ((0, x), (1, xm), (2, xp), (3, x2)):
            arrive(16 + k, bx, oth, LO, sib)
            arrive(20 + k, bx, oth, HI, sib)
        local.wait()

    return (begin, second, third, fourth, last), sent


def gather_kernel(w_ref, out_ref, local_sem, send_sem, recv_sem):
    x, y, z, core = place()
    greet([device((x + 1) % 4, y, z, core), device((x + 3) % 4, y, z, core),
           device(x, (y + 1) % 4, z, core), device(x, (y + 3) % 4, z, core), device(x, y, z, 1 - core)])
    steps, sent = gather_steps(w_ref, 0, out_ref, WIDE, CUT, local_sem, send_sem, recv_sem, 0)
    for step in steps:
        step()
    for c in sent:
        c.wait_send()


def gather_weights(packed):
    return pl.pallas_call(
        gather_kernel,
        out_shape=jax.ShapeDtypeStruct((768, WIDE), jnp.bfloat16),
        in_specs=[pl.BlockSpec(memory_space=pltpu.VMEM)],
        out_specs=pl.BlockSpec(memory_space=pltpu.VMEM),
        scratch_shapes=[
            pltpu.SemaphoreType.DMA,
            pltpu.SemaphoreType.DMA((24,)),
            pltpu.SemaphoreType.DMA((24,)),
        ],
        compiler_params=pltpu.CompilerParams(collective_id=0, has_side_effects=True),
        name="gather_weights",
    )(packed)


def add_rows(rows, step, dst, terms):
    def one(i, carry):
        at = pl.ds(pl.multiple_of(i * step, 16), step)
        total = terms[0](at).astype(jnp.float32)
        for term in terms[1:]:
            total = total + term(at).astype(jnp.float32)
        dst(at, total)
        return carry

    lax.fori_loop(0, rows // step, one, 0)


ROWS, START = (288, 288, 320), (0, 288, 576)


def layer_kernel(factor, len_ref, x_ref, ct_ref, w_ref, own_ref, taps_ref, gain_ref,
                 res_ref, gin_ref, up_ref, down_ref, rest_ref,
                 normed, invs, scaled, scaled_t, cot_t, vals, gsig, dact, gat, dfl, act, dpv, dpg,
                 mixed, dsc, kacc, kall,
                 g, cr, cs, xr, xq, xs, yr, yq, zs, zr, fin,
                 send_sem, recv_sem, zsend, zrecv, asend, arecv, wq, wlocal, wsend, wrecv):
    f32, bf = jnp.float32, jnp.bfloat16
    length = len_ref[0]
    x, y, z, core = place()
    y_lo, y_hi = y % 2, y // 2
    xp, xm, x2 = (x + 1) % 4, (x + 3) % 4, (x + 2) % 4
    yp, ym, y2 = (y + 1) % 4, (y + 3) % 4, (y + 2) % 4
    to_xp, to_xm = device(xp, y, z, core), device(xm, y, z, core)
    to_yp, to_ym = device(x, yp, z, core), device(x, ym, z, core)
    to_y2 = device(x, y2, z, core)
    to_sib = device(x, y, z, 1 - core)

    barrier = pltpu.get_barrier_semaphore()
    for partner in (to_xp, to_xm, to_yp, to_ym, to_y2, to_sib):
        pl.semaphore_signal(barrier, inc=1, device_id=partner, device_id_type=MESH)

    def hello(d, carry):
        pl.semaphore_signal(barrier, inc=1, device_id=device(x, y, (z + d) % 16, core), device_id_type=MESH)
        return carry

    lax.fori_loop(1, 16, hello, 0)
    sent = []

    def copy(index, src, dst, target):
        return pltpu.make_async_remote_copy(
            src_ref=src, dst_ref=dst, send_sem=send_sem.at[index], recv_sem=recv_sem.at[index],
            device_id=target, device_id_type=MESH)

    def send(index, src, dst, target):
        c = copy(index, src, dst, target)
        c.start()
        sent.append(c)

    def arrive(index, dst):
        copy(index, dst, dst, to_sib).wait_recv()


    def live_of(base, rows):
        return ((lax.broadcasted_iota(jnp.int32, (rows, 128), 0) + base) < length).astype(f32)


    gain = gain_ref[...]

    def norm(c, carry):
        at = pl.ds(pl.multiple_of(c * 32, 32), 32)
        v = x_ref[at, :].astype(f32)
        centred = v - jnp.mean(v, axis=1, keepdims=True)
        inv = lax.rsqrt(jnp.mean(centred * centred, axis=1, keepdims=True) + EPS)
        n = centred * inv
        normed[at, :] = n
        invs[at, :] = jnp.broadcast_to(inv, (32, 128))
        scaled[at, :] = (n * gain).astype(bf)
        return carry

    lax.fori_loop(0, 16, norm, 0)
    scaled_t[...] = scaled[...].T
    cot_t[...] = ct_ref[...].T
    for buf in (gat, dfl):
        for h in range(2):
            buf[h, pl.ds(0, 16), :] = jnp.zeros((16, 128), f32)
            buf[h, pl.ds(528, 16), :] = jnp.zeros((16, 128), f32)
    for s in range(8):
        g[2, s // 2, s % 2, 1, pl.ds(256, 64), :] = jnp.zeros((64, 128), bf)


    dot = functools.partial(lax.dot_general, preferred_element_type=f32)
    NN, NT = (((1,), (0,)), ((), ())), (((1,), (1,)), ((), ()))


    order = (x2, xp, xm, x)

    def core_start(b):
        n = pl.ds(0, ROWS[b])
        for k, bx in enumerate(order):
            send(b * 10 + k, g.at[b, bx, :, 1 - core, n], cr.at[b, bx, :, n], to_sib)

    def core_sum(b, k):
        bx, n = order[k], ROWS[b]
        arrive(b * 10 + k, cr.at[b, bx, :, pl.ds(0, n)])
        for j in range(2):
            def put(at, v):
                cs[b, bx, j, at, :] = v.astype(bf)
            add_rows(n, n // 4 if n == 320 else n // 3, put,
                     [lambda at: g[b, bx, j, core, at, :], lambda at: cr[b, bx, j, at, :]])

    def x_first(b):
        n, at = b * 10, pl.ds(0, ROWS[b])
        core_sum(b, 0)
        send(n + 4, cs.at[b, x2, 0, at], xq.at[b, 0, at], to_xp)
        send(n + 5, cs.at[b, x2, 1, at], xq.at[b, 1, at], to_xm)
        core_sum(b, 1)
        send(n + 6, cs.at[b, xp, 1, at], xr.at[b, 0, 1, at], to_xp)
        core_sum(b, 2)
        send(n + 7, cs.at[b, xm, 0, at], xr.at[b, 1, 0, at], to_xm)
        core_sum(b, 3)

    def x_second(b):
        n, rows = b * 10, pl.ds(0, ROWS[b])
        step = ROWS[b] // 4 if ROWS[b] == 320 else ROWS[b] // 3
        for q, bx, target in ((0, xp, to_xp), (1, xm, to_xm)):
            arrive(n + 4 + q, xq.at[b, q, rows])

            def put(at, v):
                cs[b, bx, q, at, :] = v.astype(bf)

            add_rows(ROWS[b], step, put, [lambda at: cs[b, bx, q, at, :], lambda at: xq[b, q, at, :]])
            send(n + 8 + q, cs.at[b, bx, q, rows], xr.at[b, q, q, rows], target)

    def x_last(b):
        n, rows = b * 10, pl.ds(0, ROWS[b])
        step = ROWS[b] // 4 if ROWS[b] == 320 else ROWS[b] // 3
        arrive(n + 6, xr.at[b, 0, 1, rows])
        arrive(n + 7, xr.at[b, 1, 0, rows])
        arrive(n + 8, xr.at[b, 0, 0, rows])
        arrive(n + 9, xr.at[b, 1, 1, rows])
        for j in range(2):
            def put(at, v):
                xs[j, pl.ds(pl.multiple_of(START[b] + at.start, 16), step), :] = v.astype(bf)
            add_rows(ROWS[b], step, put, [lambda at: cs[b, x, j, at, :], lambda at: xr[b, 0, j, at, :],
                                          lambda at: xr[b, 1, j, at, :]])

    def pack(b, part, kind):
        for h in range(2):
            for s in range(8):
                for rt in range(6):
                    t = kind * 12 + rt * 2 + h
                    per, row = ROWS[b] // 16, s * 96 + rt * 16
                    g[b, s // 2, s % 2, t // per, pl.ds(t % per * 16, 16), :] = part[
                        row : row + 16, h * 128 : h * 128 + 128]

    R = 64
    later = []
    for q in range(2):
        steps, copies = gather_steps(own_ref, q * 768, wq.at[q], 768, 384, wlocal.at[q], wsend, wrecv, q * 24)
        later.append(steps)
        sent.append(copies)
    pl.semaphore_wait(barrier, 21)
    later[0][0]()
    for b in range(3):
        if b:
            later[b - 1][4]()

        def weight(k):
            cols = pl.ds(k * 256, 256)
            return wq[b - 1, :, cols] if b else w_ref[:, cols]

        def gate(c, carry):
            base = pl.multiple_of(c * 128, 128)
            at = pl.ds(base, 128)
            live = live_of(base, 128)
            v = dot(scaled[at, :], weight(0), NN)
            sg = jax.nn.sigmoid(dot(scaled[at, :], weight(1), NN))
            vals[at, :] = v
            gsig[at, :] = sg
            dact[at, :] = dot(ct_ref[at, :], weight(2), NN)
            for h in range(2):
                cols = slice(h * 128, h * 128 + 128)
                gat[h, pl.ds(base + 16, 128), :] = (v[:, cols] * sg[:, cols] * live).astype(bf).astype(f32)
            return carry

        lax.fori_loop(0, 4, gate, 0)

        for h in range(2):
            cols = pl.ds(h * 128, 128)
            taps_cols = pl.ds(b * 256 + h * 128, 128)
            kacc[...] = jnp.zeros_like(kacc)

            def forward(c, carry):
                base = pl.multiple_of(c * R, R)
                at = pl.ds(base, R)
                live = live_of(base, R)
                total = jnp.zeros((R, 128), f32)
                for r in range(8):
                    window = gat[h, pl.ds(base + r, R + 24), :]
                    for j in range(4):
                        total = total + taps_ref[pl.ds(r + 8 * j, 1), taps_cols] * window[8 * j : 8 * j + R]
                sg = jax.nn.sigmoid(total)
                act[at, cols] = (total * sg * live).astype(bf)
                d = dact[at, cols] * live * sg * (1.0 + total * (1.0 - sg))
                dfl[h, pl.ds(base + 16, R), :] = d
                for r in range(8):
                    window = gat[h, pl.ds(base + r, R + 24), :]
                    for j in range(4):
                        prod = d * window[8 * j : 8 * j + R]
                        k = r + 8 * j
                        kacc[k] = kacc[k] + jnp.sum(prod.reshape(R // 8, 8, 128), axis=0)
                return carry

            lax.fori_loop(0, 512 // R, forward, 0)
            if b < 2:
                later[b][1 + h]()
            if b == 0 and h:
                later[1][0]()
            kall[b * 2 + h] = jnp.sum(kacc[...], axis=1)

            def backward(c, carry):
                base = pl.multiple_of(c * R, R)
                at = pl.ds(base, R)
                live = live_of(base, R)
                total = jnp.zeros((R, 128), f32)
                for r in range(8):
                    first = r if r else 8
                    window = dfl[h, pl.ds(base + first, R + 24), :]
                    for j in range(4):
                        total = total + taps_ref[pl.ds(32 - first - 8 * j, 1), taps_cols] * window[8 * j : 8 * j + R]
                total = total * live
                sg, v = gsig[at, cols], vals[at, cols]
                dpv[at, cols] = (total * sg).astype(bf)
                dpg[at, cols] = (total * v * sg * (1.0 - sg)).astype(bf)
                return carry

            lax.fori_loop(0, 512 // R, backward, 0)


            if b and not h:
                x_first(b - 1)
                if b == 2:
                    x_last(0)
        if b:
            x_second(b - 1)
        pack(b, dot(scaled_t[...], dpv[...], NN).astype(bf), 0)
        pack(b, dot(scaled_t[...], dpg[...], NN).astype(bf), 1)
        pack(b, dot(cot_t[...], act[...], NN).astype(bf), 2)
        if b < 2:
            core_start(b)
            later[b][3]()
        m = dot(act[...], weight(2), NT)
        d = dot(dpv[...], weight(0), NT) + dot(dpg[...], weight(1), NT)
        if b:
            mixed[...] += m
            dsc[...] += d
        else:
            mixed[...] = m
            dsc[...] = d

    def finish(c, gsum):
        at = pl.ds(pl.multiple_of(c * 32, 32), 32)
        ds, n = dsc[at, :], normed[at, :]
        prod = ds * n
        dn = ds * gain
        inv = invs[at, :][:, :1]
        grad = inv * (dn - jnp.mean(dn, axis=1, keepdims=True)
                      - n * jnp.mean(prod * gain, axis=1, keepdims=True))
        gin_ref[at, :] = (ct_ref[at, :].astype(f32) + grad).astype(bf)
        return gsum + jnp.sum(prod.reshape(4, 8, 768), axis=0)

    gsum = lax.fori_loop(0, 16, finish, jnp.zeros((8, 768), f32))
    gsum = jnp.sum(gsum, axis=0, keepdims=True)
    small = jnp.concatenate([kall[b] for b in range(6)], axis=1)
    small = jnp.concatenate([small, jnp.broadcast_to(gsum, (16, 768))], axis=0)
    for s in range(8):
        g[2, s // 2, s % 2, 1, pl.ds(256, 48), pl.ds(0, 96)] = small[:, s * 96 : s * 96 + 96].astype(bf)
    core_start(2)
    x_last(1)
    x_first(2)
    x_second(2)
    x_last(2)
    def part(yy, half, rows=224):
        return xs.at[yy % 2, pl.ds(pl.multiple_of((yy // 2) * 448 + half * 224, 16), rows)]

    send(30, part(y2, 0), yq.at[0], to_yp)
    send(31, part(y2, 1), yq.at[1], to_ym)
    send(32, part(yp, 1), yr.at[0, 1], to_yp)
    send(33, part(ym, 0), yr.at[1, 0], to_ym)
    arrive(30, yq.at[0])
    dst_p = part(yp, 0)

    def put_yp(at, v):
        dst_p[at, :] = v.astype(jnp.bfloat16)

    add_rows(224, 32, put_yp, [lambda at: dst_p[at, :], lambda at: yq[0, at, :]])
    send(34, part(yp, 0), yr.at[0, 0], to_yp)
    arrive(31, yq.at[1])
    dst_m = part(ym, 1)

    def put_ym(at, v):
        dst_m[at, :] = v.astype(jnp.bfloat16)

    add_rows(224, 32, put_ym, [lambda at: dst_m[at, :], lambda at: yq[1, at, :]])
    send(35, part(ym, 1), yr.at[1, 1], to_ym)
    arrive(32, yr.at[0, 1])
    arrive(33, yr.at[1, 0])
    arrive(34, yr.at[0, 0])
    arrive(35, yr.at[1, 1])
    zs[pl.ds(448, 64), :] = jnp.zeros((64, 128), jnp.bfloat16)
    for half in range(2):
        mine = part(y, half)

        def put(at, v):
            zs[pl.ds(pl.multiple_of(half * 224 + at.start, 16), 32), :] = v.astype(jnp.bfloat16)

        add_rows(224, 32, put, [lambda at: mine[at, :], lambda at: yr[0, half, at, :], lambda at: yr[1, half, at, :]])


    def piece(p):
        return pl.ds(pl.multiple_of(p * 32, 32), 32)

    def z_copy(d):
        to = (z + d) % 16
        return pltpu.make_async_remote_copy(
            src_ref=zs.at[piece(to)], dst_ref=zr.at[d], send_sem=zsend.at[d], recv_sem=zrecv.at[d],
            device_id=device(x, y, to, core), device_id_type=MESH)

    def z_start(d, carry):
        z_copy(d).start()
        return carry

    lax.fori_loop(1, 16, z_start, 0)

    def residual(c, carry):
        at = pl.ds(pl.multiple_of(c * 64, 64), 64)
        res_ref[at, :] = (x_ref[at, :].astype(f32) + mixed[at, :]).astype(bf)
        return carry

    lax.fori_loop(0, 8, residual, 0)

    def z_add(d, total):
        z_copy(d).wait_recv()
        return total + zr[d].astype(jnp.float32)

    total = lax.fori_loop(1, 16, z_add, zs[piece(z), :].astype(jnp.float32))
    mine_at = fin.at[core, y_hi]
    mine_at[piece(z), :] = total.astype(jnp.bfloat16)

    def a_copy(d, p):
        at = fin.at[core, y_hi, piece(p)]
        return pltpu.make_async_remote_copy(
            src_ref=at, dst_ref=at, send_sem=asend.at[d], recv_sem=arecv.at[d],
            device_id=device(x, y, (z + d) % 16, core), device_id_type=MESH)

    def a_start(d, carry):
        a_copy(d, z).start()
        return carry

    lax.fori_loop(1, 16, a_start, 0)

    def a_wait(d, carry):
        a_copy(d, (z + 16 - d) % 16).wait_recv()
        return carry

    lax.fori_loop(1, 16, a_wait, 0)
    both = fin.at[core, y_hi, pl.ds(0, 448)]
    send(36, both, both, to_y2)
    send(37, both, both, to_sib)
    far = fin.at[core, 1 - y_hi, pl.ds(0, 448)]
    arrive(36, far)
    send(38, far, far, to_sib)

    def z_done(d, carry):
        z_copy(d).wait_send()
        a_copy(d, z).wait_send()
        return carry

    lax.fori_loop(1, 16, z_done, 0)
    arrive(37, fin.at[1 - core, y_hi, pl.ds(0, 448)])
    arrive(38, fin.at[1 - core, 1 - y_hi, pl.ds(0, 448)])

    def tile(b, t):
        per = ROWS[b] // 16
        row = START[b] + t % per * 16
        return fin[t // per, row // 448, pl.ds(row % 448, 16), :].astype(f32) * factor

    for b in range(3):
        for h in range(2):
            at = (b * 2 + h) * 128
            for rt in range(6):
                rows = pl.ds(rt * 16, 16)
                up_ref[rows, pl.ds(at, 128)] = tile(b, rt * 2 + h)
                up_ref[rows, pl.ds(768 + at, 128)] = tile(b, 12 + rt * 2 + h)
                down_ref[rows, pl.ds(at, 128)] = tile(b, 24 + rt * 2 + h)
    for k in range(3):
        rest_ref[pl.ds(k * 16, 16), :] = tile(2, 36 + k)
    for c in sent:
        for one in c if isinstance(c, list) else [c]:
            one.wait_send()


def layer(lengths, frames, cot, full, own, taps, gain, factor):
    f32, bf = jnp.float32, jnp.bfloat16
    vmem = pl.BlockSpec(memory_space=pltpu.VMEM)
    return pl.pallas_call(
        functools.partial(layer_kernel, factor),
        out_shape=(
            jax.ShapeDtypeStruct((512, 768), bf),
            jax.ShapeDtypeStruct((512, 768), bf),
            jax.ShapeDtypeStruct((96, 1536), f32),
            jax.ShapeDtypeStruct((96, 768), f32),
            jax.ShapeDtypeStruct((48, 128), f32),
        ),
        in_specs=[pl.BlockSpec(memory_space=pltpu.SMEM)] + [vmem] * 6,
        out_specs=(vmem,) * 5,
        scratch_shapes=[
            pltpu.VMEM((512, 768), f32),
            pltpu.VMEM((512, 128), f32),
            pltpu.VMEM((512, 768), bf),
            pltpu.VMEM((768, 512), bf),
            pltpu.VMEM((768, 512), bf),
            pltpu.VMEM((512, 256), f32),
            pltpu.VMEM((512, 256), f32),
            pltpu.VMEM((512, 256), f32),
            pltpu.VMEM((2, 544, 128), f32),
            pltpu.VMEM((2, 544, 128), f32),
            pltpu.VMEM((512, 256), bf),
            pltpu.VMEM((512, 256), bf),
            pltpu.VMEM((512, 256), bf),
            pltpu.VMEM((512, 768), f32),
            pltpu.VMEM((512, 768), f32),
            pltpu.VMEM((32, 8, 128), f32),
            pltpu.VMEM((6, 32, 128), f32),
            pltpu.VMEM((3, 4, 2, 2, 320, 128), bf),
            pltpu.VMEM((3, 4, 2, 320, 128), bf),
            pltpu.VMEM((3, 4, 2, 320, 128), bf),
            pltpu.VMEM((3, 2, 2, 320, 128), bf),
            pltpu.VMEM((3, 2, 320, 128), bf),
            pltpu.VMEM((2, 896, 128), bf),
            pltpu.VMEM((2, 2, 224, 128), bf),
            pltpu.VMEM((2, 224, 128), bf),
            pltpu.VMEM((512, 128), bf),
            pltpu.VMEM((16, 32, 128), bf),
            pltpu.VMEM((2, 2, 512, 128), bf),
            pltpu.SemaphoreType.DMA((39,)),
            pltpu.SemaphoreType.DMA((39,)),
            pltpu.SemaphoreType.DMA((16,)),
            pltpu.SemaphoreType.DMA((16,)),
            pltpu.SemaphoreType.DMA((16,)),
            pltpu.SemaphoreType.DMA((16,)),
            pltpu.VMEM((2, 768, 768), bf),
            pltpu.SemaphoreType.DMA((2,)),
            pltpu.SemaphoreType.DMA((48,)),
            pltpu.SemaphoreType.DMA((48,)),
        ],
        compiler_params=pltpu.CompilerParams(
            collective_id=1, has_side_effects=True, vmem_limit_bytes=48 * 1024 * 1024),
        name="layer",
    )(lengths, frames, cot, full, own, taps, gain)


def body(frames_in, lengths, up_weight, norm_gain, conv_kernel, down_weight, cotangent):
    bf = jnp.bfloat16
    small = jnp.pad(jnp.concatenate([conv_kernel, norm_gain[None, :]], axis=0), ((0, 63), (0, 32)))
    down = down_weight.T
    parts = [a[:, at * 256 : at * 256 + 256] for b in range(3) for a, at in ((up_weight, b), (up_weight, 3 + b), (down, b))]
    full = gather_weights(jnp.concatenate(parts[:3] + [small], axis=1))
    own = jnp.concatenate(parts[3:], axis=1)
    small = full[:, 768:].reshape(8, 96, 128)[:, :33, :96].transpose(1, 0, 2).reshape(33, 768)
    small = small.astype(jnp.float32)
    factor = 1.0 / 262144.0 ** 0.5
    result, grad_in, up_total, down_total, rest = layer(
        lengths, frames_in.reshape(512, 768), cotangent.reshape(512, 768), full, own, small[:32], small[32:], factor
    )
    return (
        result.reshape(1, 512, 768),
        grad_in.reshape(1, 512, 768),
        up_total,
        rest[32, :96],
        rest[:32, :96],
        down_total.T,
    )


def solution(mesh):
    return jax.shard_map(
        body,
        mesh=mesh,
        in_specs=(
            P(("replica", "shard"), None, None),
            P(("replica", "shard")),
            P("shard", None),
            P("shard"),
            P(None, "shard"),
            P(None, "shard"),
            P(("replica", "shard"), None, None),
        ),
        out_specs=(
            P(("replica", "shard"), None, None),
            P(("replica", "shard"), None, None),
            P("shard", None),
            P("shard"),
            P(None, "shard"),
            P(None, "shard"),
        ),
        check_vma=False,
    )
```

```python
import functools

import jax
import jax.numpy as jnp
from jax import lax
from jax.experimental import pallas as pl
from jax.experimental.pallas import tpu as pltpu
from jax.sharding import PartitionSpec as P

EPS = 1e-05
WIDE = 2432
CUT = 1280
MESH = pl.DeviceIdType.MESH


def place():
    rep, sh = lax.axis_index("replica"), lax.axis_index("shard")
    z, y_hi, core = rep // 4, (rep // 2) % 2, rep % 2
    x, y_lo = sh // 2, sh % 2
    return x, y_hi * 2 + y_lo, z, core


def device(x, y, z, core):
    return ((z * 2 + y // 2) * 2 + core, x * 2 + y % 2)


def greet(partners):
    barrier = pltpu.get_barrier_semaphore()
    for partner in partners:
        pl.semaphore_signal(barrier, inc=1, device_id=partner, device_id_type=MESH)
    pl.semaphore_wait(barrier, len(partners))


def gather_kernel(w_ref, out_ref, local_sem, send_sem, recv_sem):
    x, y, z, core = place()
    y_lo = y % 2
    xp, xm, x2 = (x + 1) % 4, (x + 3) % 4, (x + 2) % 4
    yp, ym = (y + 1) % 4, (y + 3) % 4
    to_xp, to_xm = device(xp, y, z, core), device(xm, y, z, core)
    to_yp, to_ym = device(x, yp, z, core), device(x, ym, z, core)
    to_sib = device(x, y, z, 1 - core)
    greet([to_xp, to_xm, to_yp, to_ym, to_sib])

    def rows(bx, byl):
        return pl.ds(pl.multiple_of((bx * 2 + byl) * 96 + core * 48, 16), 48)

    LO, HI, ALL = pl.ds(0, CUT), pl.ds(CUT, WIDE - CUT), pl.ds(0, WIDE)
    own = pl.multiple_of((x * 2 + y_lo) * 96, 16)
    local = pltpu.make_async_copy(w_ref, out_ref.at[pl.ds(own, 96)], local_sem)
    local.start()
    mine = pl.ds(pl.multiple_of(core * 48, 16), 48)
    sent = []

    def send(index, bx, byl, cols, target, own_block=False):
        dst = out_ref.at[rows(bx, byl), cols]
        src = w_ref.at[mine, cols] if own_block else dst
        copy = pltpu.make_async_remote_copy(
            src_ref=src, dst_ref=dst, send_sem=send_sem.at[index], recv_sem=recv_sem.at[index],
            device_id=target, device_id_type=MESH)
        copy.start()
        sent.append(copy)

    def arrive(index, bx, byl, cols):
        dst = out_ref.at[rows(bx, byl), cols]
        pltpu.make_async_remote_copy(
            src_ref=dst, dst_ref=dst, send_sem=send_sem.at[index], recv_sem=recv_sem.at[index],
            device_id=to_sib, device_id_type=MESH).wait_recv()

    oth = 1 - y_lo
    send(0, x, y_lo, ALL, to_xp, True)
    send(1, x, y_lo, ALL, to_xm, True)
    send(4, x, y_lo, LO, to_yp, True)
    send(8, x, y_lo, HI, to_ym, True)
    arrive(0, xm, y_lo, ALL)
    send(2, xm, y_lo, LO, to_xp)
    send(5, xm, y_lo, LO, to_yp)
    send(9, xm, y_lo, HI, to_ym)
    arrive(1, xp, y_lo, ALL)
    send(3, xp, y_lo, HI, to_xm)
    send(6, xp, y_lo, LO, to_yp)
    send(10, xp, y_lo, HI, to_ym)
    send(12, xm, y_lo, ALL, to_sib)
    send(13, xp, y_lo, ALL, to_sib)
    arrive(4, x, oth, LO)
    send(16, x, oth, LO, to_sib)
    arrive(8, x, oth, HI)
    send(20, x, oth, HI, to_sib)
    arrive(2, x2, y_lo, LO)
    send(7, x2, y_lo, LO, to_yp)
    send(14, x2, y_lo, LO, to_sib)
    arrive(3, x2, y_lo, HI)
    send(11, x2, y_lo, HI, to_ym)
    send(15, x2, y_lo, HI, to_sib)
    for k, bx in ((1, xm), (2, xp), (3, x2)):
        arrive(4 + k, bx, oth, LO)
        send(16 + k, bx, oth, LO, to_sib)
        arrive(8 + k, bx, oth, HI)
        send(20 + k, bx, oth, HI, to_sib)

    def sib_rows(bx, byl):
        return pl.ds(pl.multiple_of((bx * 2 + byl) * 96 + (1 - core) * 48, 16), 48)

    def arrive_sib(index, bx, byl, cols):
        dst = out_ref.at[sib_rows(bx, byl), cols]
        pltpu.make_async_remote_copy(
            src_ref=dst, dst_ref=dst, send_sem=send_sem.at[index], recv_sem=recv_sem.at[index],
            device_id=to_sib, device_id_type=MESH).wait_recv()

    arrive_sib(12, xm, y_lo, ALL)
    arrive_sib(13, xp, y_lo, ALL)
    arrive_sib(14, x2, y_lo, LO)
    arrive_sib(15, x2, y_lo, HI)
    for k, bx in ((0, x), (1, xm), (2, xp), (3, x2)):
        arrive_sib(16 + k, bx, oth, LO)
        arrive_sib(20 + k, bx, oth, HI)
    for copy in sent:
        copy.wait_send()
    local.wait()


def gather_weights(packed):
    return pl.pallas_call(
        gather_kernel,
        out_shape=jax.ShapeDtypeStruct((768, WIDE), jnp.bfloat16),
        in_specs=[pl.BlockSpec(memory_space=pltpu.VMEM)],
        out_specs=pl.BlockSpec(memory_space=pltpu.VMEM),
        scratch_shapes=[
            pltpu.SemaphoreType.DMA,
            pltpu.SemaphoreType.DMA((24,)),
            pltpu.SemaphoreType.DMA((24,)),
        ],
        compiler_params=pltpu.CompilerParams(collective_id=0, has_side_effects=True),
        name="gather_weights",
    )(packed)


def add_rows(rows, step, dst, terms):
    def one(i, carry):
        at = pl.ds(pl.multiple_of(i * step, 16), step)
        total = terms[0](at).astype(jnp.float32)
        for term in terms[1:]:
            total = total + term(at).astype(jnp.float32)
        dst(at, total)
        return carry

    lax.fori_loop(0, rows // step, one, 0)


ROWS, START, QUARTER = (288, 288, 320), (0, 288, 576), (144, 80)


def layer_kernel(factor, len_ref, x_ref, ct_ref, w_ref, taps_ref, gain_ref,
                 res_ref, gin_ref, up_ref, down_ref, rest_ref,
                 normed, invs, scaled, scaled_t, cot_t, vals, gsig, dact, gat, dfl, act, dpv, dpg,
                 mixed, dsc, kacc, kall,
                 g, cr, cs, xr, xq, xs, yr, yq, zs, zr, fin,
                 send_sem, recv_sem, zsend, zrecv, asend, arecv):
    f32, bf = jnp.float32, jnp.bfloat16
    length = len_ref[0]
    x, y, z, core = place()
    y_lo, y_hi = y % 2, y // 2
    xp, xm, x2 = (x + 1) % 4, (x + 3) % 4, (x + 2) % 4
    yp, ym, y2 = (y + 1) % 4, (y + 3) % 4, (y + 2) % 4
    to_xp, to_xm = device(xp, y, z, core), device(xm, y, z, core)
    to_yp, to_ym = device(x, yp, z, core), device(x, ym, z, core)
    to_y2 = device(x, y2, z, core)
    to_sib = device(x, y, z, 1 - core)

    barrier = pltpu.get_barrier_semaphore()
    for partner in (to_xp, to_xm, to_yp, to_ym, to_y2, to_sib):
        pl.semaphore_signal(barrier, inc=1, device_id=partner, device_id_type=MESH)

    def hello(d, carry):
        pl.semaphore_signal(barrier, inc=1, device_id=device(x, y, (z + d) % 16, core), device_id_type=MESH)
        return carry

    lax.fori_loop(1, 16, hello, 0)
    sent = []

    def copy(index, src, dst, target):
        return pltpu.make_async_remote_copy(
            src_ref=src, dst_ref=dst, send_sem=send_sem.at[index], recv_sem=recv_sem.at[index],
            device_id=target, device_id_type=MESH)

    def send(index, src, dst, target):
        c = copy(index, src, dst, target)
        c.start()
        sent.append(c)

    def arrive(index, dst):
        copy(index, dst, dst, to_sib).wait_recv()


    def live_of(base, rows):
        return ((lax.broadcasted_iota(jnp.int32, (rows, 128), 0) + base) < length).astype(f32)


    gain = gain_ref[...]

    def norm(c, carry):
        at = pl.ds(pl.multiple_of(c * 32, 32), 32)
        v = x_ref[at, :].astype(f32)
        centred = v - jnp.mean(v, axis=1, keepdims=True)
        inv = lax.rsqrt(jnp.mean(centred * centred, axis=1, keepdims=True) + EPS)
        n = centred * inv
        normed[at, :] = n
        invs[at, :] = jnp.broadcast_to(inv, (32, 128))
        scaled[at, :] = (n * gain).astype(bf)
        return carry

    lax.fori_loop(0, 16, norm, 0)
    scaled_t[...] = scaled[...].T
    cot_t[...] = ct_ref[...].T
    for buf in (gat, dfl):
        for h in range(2):
            buf[h, pl.ds(0, 16), :] = jnp.zeros((16, 128), f32)
            buf[h, pl.ds(528, 16), :] = jnp.zeros((16, 128), f32)
    for s in range(8):
        g[2, s // 2, s % 2, 1, pl.ds(256, 64), :] = jnp.zeros((64, 128), bf)


    dot = functools.partial(lax.dot_general, preferred_element_type=f32)
    NN, NT = (((1,), (0,)), ((), ())), (((1,), (1,)), ((), ()))


    order = (x2, xp, xm, x)

    def core_start(b, base, first, count):
        n = pl.ds(first, count)
        for k, bx in enumerate(order):
            send(base + k, g.at[b, bx, :, 1 - core, n], cr.at[b, bx, :, n], to_sib)

    def core_sum(b, k):
        bx, n = order[k], ROWS[b]
        if b == 2:
            arrive(20 + k, cr.at[b, bx, :, pl.ds(0, 256)])
            arrive(39 + k, cr.at[b, bx, :, pl.ds(256, 64)])
        else:
            arrive(b * 10 + k, cr.at[b, bx, :, pl.ds(0, n)])
        for j in range(2):
            def put(at, v):
                cs[b, bx, j, at, :] = v.astype(bf)
            add_rows(n, n // 4 if n == 320 else n // 3, put,
                     [lambda at: g[b, bx, j, core, at, :], lambda at: cr[b, bx, j, at, :]])

    def x_first(b):
        n, at = b * 10, pl.ds(0, ROWS[b])
        core_sum(b, 0)
        send(n + 4, cs.at[b, x2, 0, at], xq.at[b, 0, at], to_xp)
        send(n + 5, cs.at[b, x2, 1, at], xq.at[b, 1, at], to_xm)
        core_sum(b, 1)
        send(n + 6, cs.at[b, xp, 1, at], xr.at[b, 0, 1, at], to_xp)
        core_sum(b, 2)
        send(n + 7, cs.at[b, xm, 0, at], xr.at[b, 1, 0, at], to_xm)
        core_sum(b, 3)

    def x_second(b):
        n, rows = b * 10, pl.ds(0, ROWS[b])
        step = ROWS[b] // 4 if ROWS[b] == 320 else ROWS[b] // 3
        for q, bx, target in ((0, xp, to_xp), (1, xm, to_xm)):
            arrive(n + 4 + q, xq.at[b, q, rows])

            def put(at, v):
                cs[b, bx, q, at, :] = v.astype(bf)

            add_rows(ROWS[b], step, put, [lambda at: cs[b, bx, q, at, :], lambda at: xq[b, q, at, :]])
            send(n + 8 + q, cs.at[b, bx, q, rows], xr.at[b, q, q, rows], target)

    def x_last(b):
        n, rows = b * 10, pl.ds(0, ROWS[b])
        step = ROWS[b] // 4 if ROWS[b] == 320 else ROWS[b] // 3
        arrive(n + 6, xr.at[b, 0, 1, rows])
        arrive(n + 7, xr.at[b, 1, 0, rows])
        arrive(n + 8, xr.at[b, 0, 0, rows])
        arrive(n + 9, xr.at[b, 1, 1, rows])
        for j in range(2):
            def put(at, v):
                xs[j, pl.ds(pl.multiple_of(START[b] + at.start, 16), step), :] = v.astype(bf)
            add_rows(ROWS[b], step, put, [lambda at: cs[b, x, j, at, :], lambda at: xr[b, 0, j, at, :],
                                          lambda at: xr[b, 1, j, at, :]])

    def pack(b, part, kind):
        for h in range(2):
            for s in range(8):
                for rt in range(6):
                    t = kind * 12 + rt * 2 + h
                    per, row = ROWS[b] // 16, s * 96 + rt * 16
                    g[b, s // 2, s % 2, t // per, pl.ds(t % per * 16, 16), :] = part[
                        row : row + 16, h * 128 : h * 128 + 128]

    R = 64
    for b in range(3):
        v_cols, g_cols, d_cols = pl.ds(b * 256, 256), pl.ds(768 + b * 256, 256), pl.ds(1536 + b * 256, 256)
        def gate(c, carry):
            base = pl.multiple_of(c * 128, 128)
            at = pl.ds(base, 128)
            live = live_of(base, 128)
            v = dot(scaled[at, :], w_ref[:, v_cols], NN)
            sg = jax.nn.sigmoid(dot(scaled[at, :], w_ref[:, g_cols], NN))
            vals[at, :] = v
            gsig[at, :] = sg
            dact[at, :] = dot(ct_ref[at, :], w_ref[:, d_cols], NN)
            for h in range(2):
                cols = slice(h * 128, h * 128 + 128)
                gat[h, pl.ds(base + 16, 128), :] = (v[:, cols] * sg[:, cols] * live).astype(bf).astype(f32)
            return carry

        lax.fori_loop(0, 4, gate, 0)

        for h in range(2):
            cols = pl.ds(h * 128, 128)
            taps_cols = pl.ds(b * 256 + h * 128, 128)
            kacc[...] = jnp.zeros_like(kacc)

            def forward(c, carry):
                base = pl.multiple_of(c * R, R)
                at = pl.ds(base, R)
                live = live_of(base, R)
                total = jnp.zeros((R, 128), f32)
                for r in range(8):
                    window = gat[h, pl.ds(base + r, R + 24), :]
                    for j in range(4):
                        total = total + taps_ref[pl.ds(r + 8 * j, 1), taps_cols] * window[8 * j : 8 * j + R]
                sg = jax.nn.sigmoid(total)
                act[at, cols] = (total * sg * live).astype(bf)
                d = dact[at, cols] * live * sg * (1.0 + total * (1.0 - sg))
                dfl[h, pl.ds(base + 16, R), :] = d
                for r in range(8):
                    window = gat[h, pl.ds(base + r, R + 24), :]
                    for j in range(4):
                        prod = d * window[8 * j : 8 * j + R]
                        k = r + 8 * j
                        kacc[k] = kacc[k] + jnp.sum(prod.reshape(R // 8, 8, 128), axis=0)
                return carry

            lax.fori_loop(0, 512 // R, forward, 0)
            kall[b * 2 + h] = jnp.sum(kacc[...], axis=1)

            def backward(c, carry):
                base = pl.multiple_of(c * R, R)
                at = pl.ds(base, R)
                live = live_of(base, R)
                total = jnp.zeros((R, 128), f32)
                for r in range(8):
                    first = r if r else 8
                    window = dfl[h, pl.ds(base + first, R + 24), :]
                    for j in range(4):
                        total = total + taps_ref[pl.ds(32 - first - 8 * j, 1), taps_cols] * window[8 * j : 8 * j + R]
                total = total * live
                sg, v = gsig[at, cols], vals[at, cols]
                dpv[at, cols] = (total * sg).astype(bf)
                dpg[at, cols] = (total * v * sg * (1.0 - sg)).astype(bf)
                return carry

            lax.fori_loop(0, 512 // R, backward, 0)


            if b and not h:
                x_first(b - 1)
                if b == 2:
                    x_last(0)
        if b:
            x_second(b - 1)
        pack(b, dot(scaled_t[...], dpv[...], NN).astype(bf), 0)
        pack(b, dot(scaled_t[...], dpg[...], NN).astype(bf), 1)
        pack(b, dot(cot_t[...], act[...], NN).astype(bf), 2)
        if b == 0:
            pl.semaphore_wait(barrier, 21)
        core_start(b, b * 10, 0, 256 if b == 2 else ROWS[b])
        m = dot(act[...], w_ref[:, d_cols], NT)
        d = dot(dpv[...], w_ref[:, v_cols], NT) + dot(dpg[...], w_ref[:, g_cols], NT)
        if b:
            mixed[...] += m
            dsc[...] += d
        else:
            mixed[...] = m
            dsc[...] = d

    def finish(c, gsum):
        at = pl.ds(pl.multiple_of(c * 32, 32), 32)
        ds, n = dsc[at, :], normed[at, :]
        prod = ds * n
        dn = ds * gain
        inv = invs[at, :][:, :1]
        grad = inv * (dn - jnp.mean(dn, axis=1, keepdims=True)
                      - n * jnp.mean(prod * gain, axis=1, keepdims=True))
        gin_ref[at, :] = (ct_ref[at, :].astype(f32) + grad).astype(bf)
        return gsum + jnp.sum(prod.reshape(4, 8, 768), axis=0)

    gsum = lax.fori_loop(0, 16, finish, jnp.zeros((8, 768), f32))
    gsum = jnp.sum(gsum, axis=0, keepdims=True)
    small = jnp.concatenate([kall[b] for b in range(6)], axis=1)
    small = jnp.concatenate([small, jnp.broadcast_to(gsum, (16, 768))], axis=0)
    for s in range(8):
        g[2, s // 2, s % 2, 1, pl.ds(256, 48), pl.ds(0, 96)] = small[:, s * 96 : s * 96 + 96].astype(bf)
    core_start(2, 39, 256, 64)

    def y_part(p, yy, half):
        q = QUARTER[p]
        return xs.at[yy % 2, pl.ds(pl.multiple_of(p * 576 + (yy // 2) * (2 * q) + half * q, 16), q)]

    def y_first(p):
        n, r = 30 + p * 13, pl.ds(p * 144, QUARTER[p])
        send(n, y_part(p, y2, 0), yq.at[0, r], to_yp)
        send(n + 1, y_part(p, y2, 1), yq.at[1, r], to_ym)
        send(n + 2, y_part(p, yp, 1), yr.at[0, 1, r], to_yp)
        send(n + 3, y_part(p, ym, 0), yr.at[1, 0, r], to_ym)

    def shifted(at, by, step):
        return pl.ds(pl.multiple_of(at.start + by, 16), step)

    def y_second(p):
        n, r = 30 + p * 13, pl.ds(p * 144, QUARTER[p])
        step = (48, 80)[p]
        for k, yy, target in ((0, yp, to_yp), (1, ym, to_ym)):
            arrive(n + k, yq.at[k, r])
            dst = y_part(p, yy, k)

            def put(at, v):
                dst[at, :] = v.astype(bf)

            add_rows(QUARTER[p], step, put,
                     [lambda at: dst[at, :], lambda at: yq[k, shifted(at, p * 144, step), :]])
            send(n + 4 + k, dst, yr.at[k, k, r], target)

    def y_last(p):
        n, r = 30 + p * 13, pl.ds(p * 144, QUARTER[p])
        step = (48, 80)[p]
        arrive(n + 2, yr.at[0, 1, r])
        arrive(n + 3, yr.at[1, 0, r])
        arrive(n + 4, yr.at[0, 0, r])
        arrive(n + 5, yr.at[1, 1, r])
        for half in range(2):
            mine = y_part(p, y, half)

            def put(at, v):
                zs[shifted(at, p * 288 + half * QUARTER[p], step), :] = v.astype(bf)

            add_rows(QUARTER[p], step, put,
                     [lambda at: mine[at, :], lambda at: yr[0, half, shifted(at, p * 144, step), :],
                      lambda at: yr[1, half, shifted(at, p * 144, step), :]])

    x_last(1)
    y_first(0)
    x_first(2)
    y_second(0)
    x_second(2)
    y_last(0)
    x_last(2)
    y_first(1)
    zs[pl.ds(448, 64), :] = jnp.zeros((64, 128), bf)
    y_second(1)
    y_last(1)

    def piece(p):
        return pl.ds(pl.multiple_of(p * 32, 32), 32)

    def z_copy(d):
        to = (z + d) % 16
        return pltpu.make_async_remote_copy(
            src_ref=zs.at[piece(to)], dst_ref=zr.at[d], send_sem=zsend.at[d], recv_sem=zrecv.at[d],
            device_id=device(x, y, to, core), device_id_type=MESH)

    def z_start(d, carry):
        z_copy(d).start()
        return carry

    lax.fori_loop(1, 16, z_start, 0)

    def residual(c, carry):
        at = pl.ds(pl.multiple_of(c * 64, 64), 64)
        res_ref[at, :] = (x_ref[at, :].astype(f32) + mixed[at, :]).astype(bf)
        return carry

    lax.fori_loop(0, 8, residual, 0)

    def z_add(d, total):
        z_copy(d).wait_recv()
        return total + zr[d].astype(jnp.float32)

    total = lax.fori_loop(1, 16, z_add, zs[piece(z), :].astype(jnp.float32))
    mine_at = fin.at[core, y_hi]
    mine_at[piece(z), :] = total.astype(jnp.bfloat16)

    def a_copy(d, p):
        at = fin.at[core, y_hi, piece(p)]
        return pltpu.make_async_remote_copy(
            src_ref=at, dst_ref=at, send_sem=asend.at[d], recv_sem=arecv.at[d],
            device_id=device(x, y, (z + d) % 16, core), device_id_type=MESH)

    def a_start(d, carry):
        a_copy(d, z).start()
        return carry

    lax.fori_loop(1, 16, a_start, 0)

    def a_wait(d, carry):
        a_copy(d, (z + 16 - d) % 16).wait_recv()
        return carry

    lax.fori_loop(1, 16, a_wait, 0)
    both = fin.at[core, y_hi, pl.ds(0, 448)]
    send(36, both, both, to_y2)
    send(37, both, both, to_sib)
    far = fin.at[core, 1 - y_hi, pl.ds(0, 448)]
    arrive(36, far)
    send(38, far, far, to_sib)

    def z_done(d, carry):
        z_copy(d).wait_send()
        a_copy(d, z).wait_send()
        return carry

    lax.fori_loop(1, 16, z_done, 0)
    arrive(37, fin.at[1 - core, y_hi, pl.ds(0, 448)])
    arrive(38, fin.at[1 - core, 1 - y_hi, pl.ds(0, 448)])

    def tile(b, t):
        per = ROWS[b] // 16
        row = START[b] + t % per * 16
        if row < 576:
            half, row = row // 288, row % 288
        else:
            half, row = (row - 576) // 160, 288 + (row - 576) % 160
        return fin[t // per, half, pl.ds(row, 16), :].astype(f32) * factor

    for b in range(3):
        for h in range(2):
            at = (b * 2 + h) * 128
            for rt in range(6):
                rows = pl.ds(rt * 16, 16)
                up_ref[rows, pl.ds(at, 128)] = tile(b, rt * 2 + h)
                up_ref[rows, pl.ds(768 + at, 128)] = tile(b, 12 + rt * 2 + h)
                down_ref[rows, pl.ds(at, 128)] = tile(b, 24 + rt * 2 + h)
    for k in range(3):
        rest_ref[pl.ds(k * 16, 16), :] = tile(2, 36 + k)
    for c in sent:
        c.wait_send()


def layer(lengths, frames, cot, full, taps, gain, factor):
    f32, bf = jnp.float32, jnp.bfloat16
    vmem = pl.BlockSpec(memory_space=pltpu.VMEM)
    return pl.pallas_call(
        functools.partial(layer_kernel, factor),
        out_shape=(
            jax.ShapeDtypeStruct((512, 768), bf),
            jax.ShapeDtypeStruct((512, 768), bf),
            jax.ShapeDtypeStruct((96, 1536), f32),
            jax.ShapeDtypeStruct((96, 768), f32),
            jax.ShapeDtypeStruct((48, 128), f32),
        ),
        in_specs=[pl.BlockSpec(memory_space=pltpu.SMEM)] + [vmem] * 5,
        out_specs=(vmem,) * 5,
        scratch_shapes=[
            pltpu.VMEM((512, 768), f32),
            pltpu.VMEM((512, 128), f32),
            pltpu.VMEM((512, 768), bf),
            pltpu.VMEM((768, 512), bf),
            pltpu.VMEM((768, 512), bf),
            pltpu.VMEM((512, 256), f32),
            pltpu.VMEM((512, 256), f32),
            pltpu.VMEM((512, 256), f32),
            pltpu.VMEM((2, 544, 128), f32),
            pltpu.VMEM((2, 544, 128), f32),
            pltpu.VMEM((512, 256), bf),
            pltpu.VMEM((512, 256), bf),
            pltpu.VMEM((512, 256), bf),
            pltpu.VMEM((512, 768), f32),
            pltpu.VMEM((512, 768), f32),
            pltpu.VMEM((32, 8, 128), f32),
            pltpu.VMEM((6, 32, 128), f32),
            pltpu.VMEM((3, 4, 2, 2, 320, 128), bf),
            pltpu.VMEM((3, 4, 2, 320, 128), bf),
            pltpu.VMEM((3, 4, 2, 320, 128), bf),
            pltpu.VMEM((3, 2, 2, 320, 128), bf),
            pltpu.VMEM((3, 2, 320, 128), bf),
            pltpu.VMEM((2, 896, 128), bf),
            pltpu.VMEM((2, 2, 224, 128), bf),
            pltpu.VMEM((2, 224, 128), bf),
            pltpu.VMEM((512, 128), bf),
            pltpu.VMEM((16, 32, 128), bf),
            pltpu.VMEM((2, 2, 512, 128), bf),
            pltpu.SemaphoreType.DMA((49,)),
            pltpu.SemaphoreType.DMA((49,)),
            pltpu.SemaphoreType.DMA((16,)),
            pltpu.SemaphoreType.DMA((16,)),
            pltpu.SemaphoreType.DMA((16,)),
            pltpu.SemaphoreType.DMA((16,)),
        ],
        compiler_params=pltpu.CompilerParams(
            collective_id=1, has_side_effects=True, vmem_limit_bytes=48 * 1024 * 1024),
        name="layer",
    )(lengths, frames, cot, full, taps, gain)


def body(frames_in, lengths, up_weight, norm_gain, conv_kernel, down_weight, cotangent):
    bf = jnp.bfloat16
    small = jnp.pad(jnp.concatenate([conv_kernel, norm_gain[None, :]], axis=0), ((0, 63), (0, 32)))
    packed = jnp.concatenate([up_weight, down_weight.T, small], axis=1)
    full = gather_weights(packed)
    small = full[:, 2304:].reshape(8, 96, 128)[:, :33, :96].transpose(1, 0, 2).reshape(33, 768)
    small = small.astype(jnp.float32)
    factor = 1.0 / 262144.0 ** 0.5
    result, grad_in, up_total, down_total, rest = layer(
        lengths, frames_in.reshape(512, 768), cotangent.reshape(512, 768), full, small[:32], small[32:], factor
    )
    return (
        result.reshape(1, 512, 768),
        grad_in.reshape(1, 512, 768),
        up_total,
        rest[32, :96],
        rest[:32, :96],
        down_total.T,
    )


def solution(mesh):
    return jax.shard_map(
        body,
        mesh=mesh,
        in_specs=(
            P(("replica", "shard"), None, None),
            P(("replica", "shard")),
            P("shard", None),
            P("shard"),
            P(None, "shard"),
            P(None, "shard"),
            P(("replica", "shard"), None, None),
        ),
        out_specs=(
            P(("replica", "shard"), None, None),
            P(("replica", "shard"), None, None),
            P("shard", None),
            P("shard"),
            P(None, "shard"),
            P(None, "shard"),
        ),
        check_vma=False,
    )
```
